256 devices in a mesh: ctx: 8 (over x, core), tp: 32 (over y, z).
Axes of the slice: x: 4, y: 4, z: 8, core: 2. Of those that a mesh axis runs over, the one named last changes fastest.
Arguments:
- tokens: bfloat16 [1024, 8192], P('ctx', 'tp'), may hold values from -6 to 6
- in_weight: bfloat16 [8192, 3, 8192], P(None, None, 'tp'), may hold values from -0.0625 to 0.0625
- filter_taps: float32 [3, 3, 8192], P(None, None, 'tp'), may hold values from -2.4 to 2.4
- decay_rate: float32 [16, 8192], P(None, 'tp'), may hold values from 0.0001953125 to 0.08, as said below
- residue: float32 [16, 8192], P(None, 'tp'), may hold values from -80 to 80
Outputs:
- gated: bfloat16 [1024, 8192], P('ctx', 'tp')
The draws below stay inside these ranges and needn't reach their ends.
Inputs may be any that keep to these rules, and one draw needn't show every extreme that they name: `decay_rate`: every decay rate lies between 0.2 / 1024 and 0.08.
All inputs are finite; a program needn't handle non-finite values.
Results may differ from the reference program's by a relative error of at most 0.015.
Values may be sent and summed in bfloat16 or wider, within the bound.
A program may use at most 128 MiB of HBM per device.

```python
import jax
import jax.numpy as jnp
from jax import lax

D = 8192
ORDER = 16
TAPS = 3
BLOCK = 128
SEQ = 1024


def group_law(key):
    groups = ORDER // 4
    spacing = jax.random.uniform(jax.random.fold_in(key, 101), (groups, 1, D), jnp.float32, 0.095, 0.18)
    place = jax.random.uniform(jax.random.fold_in(key, 102), (groups, 1, D), jnp.float32)
    size = jax.random.uniform(jax.random.fold_in(key, 103), (groups, 1, D), jnp.float32, 0.3, 0.7)
    flips = jax.random.uniform(jax.random.fold_in(key, 104), (groups, 1, D), jnp.float32)
    sign = jnp.where(flips < 0.5, -1.0, 1.0).astype(jnp.float32)
    return (spacing, place, size, sign)


def draw_decay_rate(key, part):
    spacing, place, size, sign = group_law(key)
    low_end = jnp.log(0.2 / SEQ)
    high_end = jnp.log(0.08) - 3.0 * spacing
    base = low_end + (high_end - low_end) * place
    steps_in_group = jnp.arange(4, dtype=jnp.float32)[None, :, None]
    rates = jnp.exp(base + spacing * steps_in_group)
    return rates.reshape(ORDER, D).astype(jnp.float32)


def draw_residue(key, part):
    spacing, place, size, sign = group_law(key)
    pattern = jnp.array([1.0, -1.0, -1.0, 1.0], jnp.float32)[None, :, None]
    values = sign * size / (spacing * spacing) * pattern
    return values.reshape(ORDER, D).astype(jnp.float32)


def block_scale(key, dims, cuts, low, top_value):
    gain = 1.0
    for dim, shards_of in cuts:
        steps = jax.random.uniform(jax.random.fold_in(jax.random.fold_in(key, 6), dim), (shards_of,), jnp.float32, low / len(cuts), top_value / len(cuts))
        gain = gain * jnp.repeat(jnp.exp(steps), dims[dim] // shards_of).reshape((-1,) + (1,) * (len(dims) - 1 - dim))
    return gain


def noise(key, shape, scale, reach, pieces=(), held_as=jnp.bfloat16):
    gain = block_scale(key, shape, pieces, -0.22, 0.18) if pieces else 1.0
    drawn = jax.random.normal(key, shape, jnp.float32) * scale * gain
    return jnp.minimum(jnp.maximum(drawn, -reach), reach).astype(held_as)


def setup_inputs(seed: int = 0) -> dict:
    keys = jax.random.split(jax.random.key(seed), 6)
    return {
        "tokens": noise(keys[0], (SEQ, D), 1.0, 6.0, ((0, 8), (1, 32))),
        "in_weight": noise(keys[1], (D, 3, D), D ** -0.5, 0.0625, ((2, 32),)),
        "filter_taps": noise(keys[2], (TAPS, 3, D), 0.4, 2.4, ((2, 32),), jnp.float32),
        "decay_rate": draw_decay_rate(jax.random.fold_in(keys[5], 71), 0),
        "residue": draw_residue(jax.random.fold_in(keys[5], 71), 0),
    }


def reference(tokens, in_weight, filter_taps, decay_rate, residue):
    seq_len = tokens.shape[0]
    weight_flat = in_weight.reshape(D, 3 * D)
    projected = jnp.dot(tokens, weight_flat, preferred_element_type=jnp.float32)
    projected = projected.astype(jnp.bfloat16).reshape(seq_len, 3, D)
    lead_rows = TAPS - 1
    padded = jnp.concatenate([jnp.zeros((lead_rows, 3, D), projected.dtype), projected], axis=0)
    features = jnp.zeros((seq_len, 3, D), jnp.float32)
    for lag_index in range(TAPS):
        window = padded[lead_rows - lag_index:lead_rows - lag_index + seq_len].astype(jnp.float32)
        features = features + filter_taps[lag_index] * window
    query_part = features[:, 0]
    source = features[:, 1] * features[:, 2]
    coeffs = residue * jnp.sqrt(1.0 - jnp.exp(-2.0 * decay_rate))
    offsets = jnp.arange(BLOCK, dtype=jnp.float32)
    kernel = lax.optimization_barrier(jnp.sum(coeffs[None] * jnp.exp(-decay_rate[None] * offsets[:, None, None]), axis=1))
    gap_counts = jnp.arange(BLOCK)[:, None] - jnp.arange(BLOCK)[None, :]
    toeplitz = jnp.where((gap_counts >= 0)[:, :, None], kernel[jnp.maximum(gap_counts, 0)], 0.0)
    end_weights = jnp.exp(-decay_rate[None] * (BLOCK - 1.0 - offsets)[:, None, None])
    read_weights = coeffs[None] * jnp.exp(-decay_rate[None] * (offsets + 1.0)[:, None, None])
    block_decay = jnp.exp(-decay_rate * BLOCK)
    blocks = source.reshape(seq_len // BLOCK, BLOCK, D)

    def advance(carry_state, block_rows):
        inner_part = jnp.einsum('ijc,jc->ic', toeplitz, block_rows, precision=lax.Precision.HIGHEST)
        carried = jnp.einsum('inc,nc->ic', read_weights, carry_state, precision=lax.Precision.HIGHEST)
        state_next = block_decay * carry_state + jnp.einsum('jnc,jc->nc', end_weights, block_rows, precision=lax.Precision.HIGHEST)
        return (state_next, inner_part + carried)
    _, outputs = lax.scan(advance, jnp.zeros((ORDER, D), jnp.float32), blocks)
    response = outputs.reshape(seq_len, D)
    return (query_part * response).astype(jnp.bfloat16)
```

```python
import jax
import jax.numpy as jnp
from jax import lax
from jax.experimental import pallas as pl
from jax.experimental.pallas import tpu as pltpu
from jax.sharding import PartitionSpec as P

MESH = pl.DeviceIdType.MESH
PIECES = 2
LATENCY = 1.5
LEAD = 1.0
AHEAD = 12
LANES = 256
ROWS = 128
MODES = 16
HALO = 8


def torus(tp):
    return (4, 8) if tp == 32 else (2, tp // 2)


def plan(sizes, pieces):
    wide, deep = sizes
    steps = ((1, 0), (-1, 0), (0, 1), (0, -1))

    def far(v):
        return min(v[0], wide - v[0]) + min(v[1], deep - v[1])

    arrival = [{(0, 0): 0.0} for _ in range(pieces)]
    free = [0.0] * 4
    sends = []
    while len(sends) < pieces * (wide * deep - 1):
        choices = []
        for d, (dy, dz) in enumerate(steps):
            for h in range(pieces):
                for v, at in arrival[h].items():
                    w = ((v[0] + dy) % wide, (v[1] + dz) % deep)
                    if w not in arrival[h]:
                        start = max(at, free[d])
                        side = (h + d) % 2
                        choices.append((start, -far(w), side, h, d, v, w))
        start, _, _, h, d, v, w = min(choices)
        free[d] = start + 1.0
        arrival[h][w] = start + 1.0 + LATENCY
        sends.append((start, d, h, v, w))
    return sends, arrival


def body(sizes, tokens, weight, taps_hbm, decay_hbm, residue_hbm, out, buf, wbuf, acc, taps, decay, residue,
         reversed_fall, read, kern, kern_rows, proj, source, shifted, inner, query, pay, inbox,
         local_sem, weight_sem, send_sem, recv_sem, pay_send, pay_recv):
    wide, deep = sizes
    count = wide * deep
    ctx = lax.axis_size("ctx")
    me = lax.axis_index("tp")
    c = lax.axis_index("ctx")
    my, mz = me // deep, lax.rem(me, deep)
    sends, arrival = plan(sizes, PIECES)
    piece = ROWS // PIECES

    neighbours = (
        lax.rem(my + 1, wide) * deep + mz,
        lax.rem(my + wide - 1, wide) * deep + mz,
        my * deep + lax.rem(mz + 1, deep),
        my * deep + lax.rem(mz + deep - 1, deep),
    )

    def slot(v):
        return v[0] * deep + v[1]

    ready = sorted(
        ((max(arrival[h][v] for h in range(PIECES)), slot(v), v) for v in arrival[0]),
    )
    blocks = [v for _, _, v in ready]

    def weight_copy(v):
        owner = lax.rem(my - v[0] + wide, wide) * deep + lax.rem(mz - v[1] + deep, deep)
        rows = pl.ds(pl.multiple_of(owner * LANES, LANES), LANES)
        return pltpu.make_async_copy(weight.at[:, rows, :], wbuf.at[slot(v)], weight_sem.at[slot(v)])

    own = pltpu.make_async_copy(tokens, buf.at[0], local_sem.at[0])
    small = [
        pltpu.make_async_copy(taps_hbm, taps, local_sem.at[1]),
        pltpu.make_async_copy(decay_hbm, decay, local_sem.at[2]),
        pltpu.make_async_copy(residue_hbm, residue, local_sem.at[3]),
    ]

    inbox[...] = jnp.zeros_like(inbox)
    barrier = pltpu.get_barrier_semaphore()
    for n in neighbours:
        pl.semaphore_signal(barrier, inc=1, device_id={"tp": n}, device_id_type=MESH)
    for d in range(1, ctx):
        @pl.when(c - d >= 0)
        def _(d=d):
            pl.semaphore_signal(barrier, inc=1, device_id={"ctx": c - d}, device_id_type=MESH)
    own.start()
    for copy in small:
        copy.start()
    for v in blocks[:AHEAD]:
        weight_copy(v).start()
    proj[:, 0:HALO, :] = jnp.zeros((3, HALO, LANES), jnp.float32)
    source[0:HALO, :] = jnp.zeros((HALO, LANES), jnp.float32)
    kern[...] = jnp.zeros_like(kern)
    pl.semaphore_wait(barrier, 4 + ctx - 1 - c)

    def piece_copy(index, d, h, v, w):
        rows = pl.ds(h * piece, piece)
        src = tokens.at[rows] if v == (0, 0) else buf.at[slot(v), rows]
        return pltpu.make_async_remote_copy(
            src_ref=src,
            dst_ref=buf.at[slot(w), rows],
            send_sem=send_sem.at[index],
            recv_sem=recv_sem.at[h * count + slot(w)],
            device_id={"tp": neighbours[d]},
            device_id_type=MESH,
        )

    came = {}
    for index, (start, d, h, v, w) in enumerate(sends):
        came[(h, w)] = (index, d, h, v, w)
    arrived = {(h, (0, 0)) for h in range(PIECES)}

    def await_piece(h, v):
        if (h, v) not in arrived:
            arrived.add((h, v))
            piece_copy(*came[(h, v)]).wait_recv()

    def table(n):
        if n == 0:
            for copy in small:
                copy.wait()
        rate = decay[n : n + 1, :]
        coeff = residue[n : n + 1, :] * jnp.sqrt(1.0 - jnp.exp(-2.0 * rate))
        at = lax.broadcasted_iota(jnp.int32, (ROWS, LANES), 0).astype(jnp.float32)
        falling = jnp.exp(-rate * at)
        reversed_fall[n] = jnp.exp(-rate * (ROWS - 1.0 - at))
        read[n] = (coeff * jnp.exp(-rate)) * falling
        kern[HALO:, :] += coeff * falling

    def spread():
        @pl.loop(0, ROWS // 8)
        def _(q):
            rows = kern[pl.ds(pl.multiple_of(q * 8 + HALO, 8), 8), :]
            for r in range(8):
                kern_rows[r, q] = jnp.broadcast_to(rows[r : r + 1, :], (8, LANES))

    def multiply(order, v):
        if v == (0, 0):
            own.wait()
        for h in range(PIECES):
            await_piece(h, v)
        weight_copy(v).wait()
        lhs = buf[slot(v)]
        for s in range(3):
            part = jnp.dot(lhs, wbuf[slot(v), s], preferred_element_type=jnp.float32)
            if order == 0:
                acc[s] = part
            else:
                acc[s] += part

    events = [(max(arrival[s[2]][s[3]], s[0] - LEAD), 0, i) for i, s in enumerate(sends)]
    events += [(at, 1, i) for i, (at, _, _) in enumerate(ready)]
    tables = 0
    for at, kind, i in sorted(events):
        if kind == 0:
            start, d, h, v, w = sends[i]
            await_piece(h, v)
            piece_copy(i, d, h, v, w).start()
        else:
            if i + AHEAD < count:
                weight_copy(blocks[i + AHEAD]).start()
            multiply(i, blocks[i])
            if i < count - 1:
                for _ in range(-(-MODES * (i + 1) // (count - 4)) - tables):
                    if tables < MODES:
                        table(tables)
                        tables += 1
                        if tables == MODES:
                            spread()

    def features(s, first, rows):
        at = first + HALO
        total = taps[0, s : s + 1, :] * proj[s, at : at + rows, :]
        total = total + taps[1, s : s + 1, :] * proj[s, at - 1 : at - 1 + rows, :]
        return total + taps[2, s : s + 1, :] * proj[s, at - 2 : at - 2 + rows, :]

    for s in range(3):
        proj[s, HALO:, :] = acc[s].astype(jnp.bfloat16).astype(jnp.float32)
    rows_in = lax.broadcasted_iota(jnp.int32, (ROWS, LANES), 0)
    late = jnp.where(rows_in >= 2, features(1, 0, ROWS) * features(2, 0, ROWS), 0.0)
    source[HALO:, :] = late
    for n in range(MODES):
        pay[n : n + 1, :] = jnp.sum(reversed_fall[n] * late, axis=0, keepdims=True)
    end = HALO + ROWS
    pay[16:18, :] = proj[1, HALO : HALO + 2, :]
    pay[18:20, :] = proj[1, end - 2 : end, :]
    pay[20:22, :] = proj[2, HALO : HALO + 2, :]
    pay[22:24, :] = proj[2, end - 2 : end, :]
    pay[24:26, :] = proj[0, end - 2 : end, :]
    pay[26:32, :] = jnp.zeros((6, LANES), jnp.float32)

    def pay_copy(d):
        rows = pl.ds(0, 32 if d == 1 else 24)
        return pltpu.make_async_remote_copy(
            src_ref=pay.at[rows],
            dst_ref=inbox.at[d - 1, rows],
            send_sem=pay_send.at[d - 1],
            recv_sem=pay_recv.at[d - 1],
            device_id={"ctx": lax.rem(c + d, ctx)},
            device_id_type=MESH,
        )

    for d in range(1, ctx):
        @pl.when(c + d < ctx)
        def _(d=d):
            pay_copy(d).start()

    query[...] = features(0, 0, ROWS)
    for r in range(8):
        shifted[r] = source[HALO - r : HALO - r + ROWS, :]
    inner[...] = jnp.zeros_like(inner)

    @pl.loop(0, 8)
    def _(r):
        for half in range(LANES // 128):
            lanes = slice(half * 128, half * 128 + 128)
            late_rows = [shifted[r, 8 * i : 8 * i + 8, lanes] for i in range(ROWS // 8)]
            sums = [inner[8 * i : 8 * i + 8, lanes] for i in range(ROWS // 8)]
            for q in range(ROWS // 8):
                tap = kern_rows[r, q, :, lanes]
                for i in range(q, ROWS // 8):
                    sums[i] = sums[i] + tap * late_rows[i - q]
            for i in range(ROWS // 8):
                inner[8 * i : 8 * i + 8, lanes] = sums[i]

    rates = decay[...]
    over = jnp.exp(-rates * ROWS)
    from_first = jnp.exp(-rates * (ROWS - 1.0))
    from_second = jnp.exp(-rates * (ROWS - 2.0))

    for d in range(1, ctx):
        @pl.when(c - d >= 0)
        def _(d=d):
            pay_copy(d).wait_recv()

    def lead(d, s):
        base = 16 + 4 * (s - 1)
        first = inbox[d - 1, base : base + 1, :]
        second = inbox[d - 1, base + 1 : base + 2, :]
        if d < ctx - 1:
            before = inbox[d, base + 2 : base + 3, :]
            last = inbox[d, base + 3 : base + 4, :]
        else:
            before = last = jnp.zeros((1, LANES), jnp.float32)
        t0, t1, t2 = (taps[j, s : s + 1, :] for j in range(3))
        return t0 * first + t1 * last + t2 * before, t0 * second + t1 * first + t2 * last

    state = jnp.zeros((MODES, LANES), jnp.float32)
    for d in range(ctx - 1, 0, -1):
        key_first, key_second = lead(d, 1)
        value_first, value_second = lead(d, 2)
        left = inbox[d - 1, 0:MODES, :]
        left = left + from_first * (key_first * value_first) + from_second * (key_second * value_second)
        state = over * state + left

    proj[0, HALO - 2 : HALO, :] = inbox[0, 24:26, :]
    proj[1, HALO - 2 : HALO, :] = inbox[0, 18:20, :]
    proj[2, HALO - 2 : HALO, :] = inbox[0, 22:24, :]
    query[0:8, :] = features(0, 0, 8)
    early = features(1, 0, 8) * features(2, 0, 8)

    response = inner[...]
    response = response + kern[HALO:, :] * early[0:1, :] + kern[HALO - 1 : HALO - 1 + ROWS, :] * early[1:2, :]
    for n in range(MODES):
        response = response + read[n] * state[n : n + 1, :]
    out[...] = (query[...] * response).astype(out.dtype)

    for d in range(1, ctx):
        @pl.when(c + d < ctx)
        def _(d=d):
            pay_copy(d).wait_send()
    for i, (start, d, h, v, w) in enumerate(sends):
        piece_copy(i, d, h, v, w).wait_send()


def on_device(tokens, in_weight, filter_taps, decay_rate, residue):
    count = lax.axis_size("tp")
    ctx = lax.axis_size("ctx")
    sizes = torus(count)
    weight = jnp.transpose(in_weight, (1, 0, 2))
    hbm = pl.BlockSpec(memory_space=pltpu.MemorySpace.HBM)
    f32 = jnp.float32
    scratch = [
        pltpu.VMEM((count, ROWS, LANES), jnp.bfloat16),
        pltpu.VMEM((count, 3, LANES, LANES), jnp.bfloat16),
        pltpu.VMEM((3, ROWS, LANES), f32),
        pltpu.VMEM((3, 3, LANES), f32),
        pltpu.VMEM((MODES, LANES), f32),
        pltpu.VMEM((MODES, LANES), f32),
        pltpu.VMEM((MODES, ROWS, LANES), f32),
        pltpu.VMEM((MODES, ROWS, LANES), f32),
        pltpu.VMEM((HALO + ROWS, LANES), f32),
        pltpu.VMEM((8, ROWS // 8, 8, LANES), f32),
        pltpu.VMEM((3, HALO + ROWS, LANES), f32),
        pltpu.VMEM((HALO + ROWS, LANES), f32),
        pltpu.VMEM((8, ROWS, LANES), f32),
        pltpu.VMEM((ROWS, LANES), f32),
        pltpu.VMEM((ROWS, LANES), f32),
        pltpu.VMEM((32, LANES), f32),
        pltpu.VMEM((ctx - 1, 32, LANES), f32),
        pltpu.SemaphoreType.DMA((4,)),
        pltpu.SemaphoreType.DMA((count,)),
        pltpu.SemaphoreType.DMA((PIECES * (count - 1),)),
        pltpu.SemaphoreType.DMA((PIECES * count,)),
        pltpu.SemaphoreType.DMA((ctx - 1,)),
        pltpu.SemaphoreType.DMA((ctx - 1,)),
    ]

    def kernel(*refs):
        body(sizes, *refs)

    return pl.pallas_call(
        kernel,
        out_shape=jax.ShapeDtypeStruct((ROWS, LANES), jnp.bfloat16),
        in_specs=[hbm] * 5,
        out_specs=pl.BlockSpec(memory_space=pltpu.MemorySpace.VMEM),
        scratch_shapes=scratch,
        compiler_params=pltpu.CompilerParams(
            collective_id=0, has_side_effects=True, vmem_limit_bytes=56 * 1024 * 1024
        ),
        name="hyena",
    )(tokens, weight, filter_taps, decay_rate, residue)


def solution(mesh):
    return jax.shard_map(
        on_device,
        mesh=mesh,
        in_specs=(
            P("ctx", "tp"),
            P(None, None, "tp"),
            P(None, None, "tp"),
            P(None, "tp"),
            P(None, "tp"),
        ),
        out_specs=P("ctx", "tp"),
        check_vma=False,
    )
```

```python
import jax
import jax.numpy as jnp
from jax import lax
from jax.experimental import pallas as pl
from jax.experimental.pallas import tpu as pltpu
from jax.sharding import PartitionSpec as P

MESH = pl.DeviceIdType.MESH
PIECES = 2
PLAN = (
    (1, 0, 0, 1, 0), (0, 0, 0, 0, -1), (0, 0, 0, 0, 1), (0, 0, 0, -1, 0), (0, 0), (1, 0, 0, -1, 0), (1, 0, 0, 0, 1),
    (1, 0, 0, 0, -1), (0, 0, 0, 1, 0), (1, 0, 0, 0, -2), (0, 0, 0, 0, 2), (0, 3, 0, 0, -1), (0, 0, 1, -1, 0),
    (0, 0, 7, 1, 0), (1, 1, 0, 0, 1), (0, 0, 7, 0, -1), (1, 0, 7, 1, 0), (1, 0, 7, -1, 0), (1, 3, 0, 0, 1), (0, 1),
    (0, 7), (1, 0), (3, 0), (0, 1, 0, 0, 1), (0, 1, 0, 1, 0), (1, 3, 0, -1, 0), (1, 0, 6, 0, -1), (1, 0, 6, -1, 0),
    (0, 0, 2, 0, 1), (1, 0, 6, 1, 0), (1, 0, 6, 0, -2), (0, 0, 2, 1, 0), (0, 0, 2, -1, 0), (1, 1, 1, 0, 1),
    (1, 1, 1, 1, 0), (0, 3, 7, -1, 0), (1, 3, 1, 0, 1), (0, 0, 6, 0, -1), (1, 3, 7, -1, 0), (0, 0, 6, 1, 0), (0, 6),
    (1, 7), (3, 1), (3, 7), (0, 3, 7, 0, -1), (0, 2, 0, 0, 1), (1, 1), (2, 0), (1, 0, 5, -1, 0), (1, 0, 5, 1, 0),
    (0, 0, 3, 0, 1), (0, 0, 3, -1, 0), (1, 3, 6, 0, -2), (0, 0, 3, 1, 0), (0, 1, 2, 0, 2), (0, 3, 2, -1, 0),
    (1, 1, 2, 1, 0), (1, 2), (1, 0, 4, 1, 0), (0, 2, 7, 0, -1), (1, 3, 2, 0, 1), (3, 2), (0, 0, 5, -1, 0), (0, 5),
    (0, 0, 5, 1, 0), (1, 2, 7, 0, -1), (1, 6), (2, 7), (1, 1, 2, 0, 1), (1, 0, 4, 0, -1), (2, 1), (3, 6),
    (1, 3, 2, 1, 0), (1, 3, 5, -1, 0), (0, 2, 7, 0, -2), (0, 4), (0, 3, 3, 0, 1), (0, 3, 3, -1, 0), (1, 3, 4, -1, 0),
    (0, 1, 4, 1, 0), (1, 2, 2, 0, 1), (2, 2), (1, 4), (3, 5), (3, 3), (2, 6), (1, 5), (1, 3), (0, 3), (0, 2), (3, 4),
    (2, 5), (2, 3), (2, 4),
)
AHEAD = 12
FIRST_TABLE = 2
LANES = 256
ROWS = 128
MODES = 16
HALO = 8


WIDE, DEEP = 4, 8
GROUP = 4


def body(tokens, weight, taps_hbm, decay_hbm, residue_hbm, out, buf, wbuf, acc, taps, decay, residue,
         reversed_fall, read, kern, kern_rows, proj, source, shifted, inner, query, pay, inbox,
         local_sem, weight_sem, send_sem, recv_sem, pay_send, pay_recv):
    count = WIDE * DEEP
    ctx = lax.axis_size("ctx")
    me = lax.axis_index("tp")
    c = lax.axis_index("ctx")
    my, mz = me // DEEP, lax.rem(me, DEEP)
    sends = [p for p in PLAN if len(p) == 5]
    blocks = [p for p in PLAN if len(p) == 2]
    piece = ROWS // PIECES
    turn = 1

    def at_offset(dy, dz):
        return lax.rem(my + turn * dy + 2 * WIDE, WIDE) * DEEP + lax.rem(mz + turn * dz + 2 * DEEP, DEEP)

    steps = sorted({p[3:] for p in sends})
    slots = {v: i for i, v in enumerate(blocks)}

    def slot(v):
        return slots[v]

    def weight_copy(v):
        rows = pl.ds(pl.multiple_of(at_offset(-v[0], -v[1]) * LANES, LANES), LANES)
        return pltpu.make_async_copy(weight.at[:, rows, :], wbuf.at[slot(v)], weight_sem.at[slot(v) // GROUP])

    def weight_wait(group):
        some = wbuf.at[pl.ds(group * GROUP, GROUP)]
        pltpu.make_async_copy(some, some, weight_sem.at[group]).wait()

    own = pltpu.make_async_copy(tokens, buf.at[0], local_sem.at[0])
    small = [
        pltpu.make_async_copy(taps_hbm, taps, local_sem.at[1]),
        pltpu.make_async_copy(decay_hbm, decay, local_sem.at[2]),
        pltpu.make_async_copy(residue_hbm, residue, local_sem.at[3]),
    ]

    barrier = pltpu.get_barrier_semaphore()
    for dy, dz in steps:
        pl.semaphore_signal(barrier, inc=1, device_id={"tp": at_offset(-dy, -dz)}, device_id_type=MESH)
    inbox[...] = jnp.zeros_like(inbox)
    for d in range(1, ctx):
        @pl.when(c - d >= 0)
        def _(d=d):
            pl.semaphore_signal(barrier, inc=1, device_id={"ctx": c - d}, device_id_type=MESH)
    own.start()
    for copy in small:
        copy.start()
    for v in blocks[:AHEAD]:
        weight_copy(v).start()
    proj[:, 0:HALO, :] = jnp.zeros((3, HALO, LANES), jnp.float32)
    source[0:HALO, :] = jnp.zeros((HALO, LANES), jnp.float32)
    kern[...] = jnp.zeros_like(kern)
    pl.semaphore_wait(barrier, len(steps) + ctx - 1 - c)

    passed = {(h, (y, z)) for h, y, z, _, _ in sends}
    kept = sorted(p for p in passed if p[1] != (0, 0))
    order_of = {p: i for i, p in enumerate(kept)}
    leaves = {v: [h for h in range(PIECES) if (h, v) not in passed] for v in blocks}

    def recv_at(h, w):
        return recv_sem.at[order_of[h, w] if (h, w) in passed else len(kept) + slot(w)]

    def piece_copy(step, h, v, w):
        rows = pl.ds(h * piece, piece)
        src = tokens.at[rows] if v == (0, 0) else buf.at[slot(v), rows]
        return pltpu.make_async_remote_copy(
            src_ref=src,
            dst_ref=buf.at[slot(w), rows],
            send_sem=send_sem.at[0],
            recv_sem=recv_at(h, w),
            device_id={"tp": at_offset(*step)},
            device_id_type=MESH,
        )

    arrived = {(h, (0, 0)) for h in range(PIECES)}

    def await_piece(h, v):
        if (h, v) not in arrived:
            arrived.add((h, v))
            ref = buf.at[slot(v), pl.ds(h * piece, piece)]
            pltpu.make_async_copy(ref, ref, recv_at(h, v)).wait()

    def await_leaves(v):
        if leaves[v]:
            ref = buf.at[slot(v), pl.ds(0, piece * len(leaves[v]))]
            pltpu.make_async_copy(ref, ref, recv_at(leaves[v][0], v)).wait()

    def table(n):
        if n == 0:
            for copy in small:
                copy.wait()
        rate = decay[n : n + 1, :]
        coeff = residue[n : n + 1, :] * jnp.sqrt(1.0 - jnp.exp(-2.0 * rate))
        at = lax.broadcasted_iota(jnp.int32, (ROWS, LANES), 0).astype(jnp.float32)
        falling = jnp.exp(-rate * at)
        reversed_fall[n] = jnp.exp(-rate * (ROWS - 1.0 - at))
        read[n] = (coeff * jnp.exp(-rate)) * falling
        kern[HALO:, :] += coeff * falling

    def spread():
        @pl.loop(0, ROWS // 8)
        def _(q):
            rows = kern[pl.ds(pl.multiple_of(q * 8 + HALO, 8), 8), :]
            for r in range(8):
                kern_rows[r, q] = jnp.broadcast_to(rows[r : r + 1, :], (8, LANES))

    def multiply(order, v):
        if v == (0, 0):
            own.wait()
        for h in range(PIECES):
            if (h, v) in passed:
                await_piece(h, v)
        await_leaves(v)
        if order % GROUP == 0:
            weight_wait(order // GROUP)
        lhs = buf[slot(v)]
        for s in range(3):
            part = jnp.dot(lhs, wbuf[slot(v), s], preferred_element_type=jnp.float32)
            if order == 0:
                acc[s] = part
            else:
                acc[s] += part

    tables = 0
    for p in PLAN:
        if len(p) == 5:
            h, v, step = p[0], p[1:3], p[3:]
            w = (v[0] + step[0]) % WIDE, (v[1] + step[1]) % DEEP
            await_piece(h, v)
            piece_copy(step, h, v, w).start()
            continue
        i = slot(p)
        if i + AHEAD < count:
            weight_copy(blocks[i + AHEAD]).start()
        multiply(i, p)
        if tables < MODES and i >= FIRST_TABLE:
            table(tables)
            tables += 1
            if tables == MODES:
                spread()

    def features(s, first, rows):
        at = first + HALO
        total = taps[0, s : s + 1, :] * proj[s, at : at + rows, :]
        total = total + taps[1, s : s + 1, :] * proj[s, at - 1 : at - 1 + rows, :]
        return total + taps[2, s : s + 1, :] * proj[s, at - 2 : at - 2 + rows, :]

    for s in range(3):
        proj[s, HALO:, :] = acc[s].astype(jnp.bfloat16).astype(jnp.float32)
    rows_in = lax.broadcasted_iota(jnp.int32, (ROWS, LANES), 0)
    late = jnp.where(rows_in >= 2, features(1, 0, ROWS) * features(2, 0, ROWS), 0.0)
    source[HALO:, :] = late
    for n in range(MODES):
        pay[n : n + 1, :] = jnp.sum(reversed_fall[n] * late, axis=0, keepdims=True)
    end = HALO + ROWS
    pay[16:18, :] = proj[1, HALO : HALO + 2, :]
    pay[18:20, :] = proj[1, end - 2 : end, :]
    pay[20:22, :] = proj[2, HALO : HALO + 2, :]
    pay[22:24, :] = proj[2, end - 2 : end, :]
    pay[24:26, :] = proj[0, end - 2 : end, :]
    pay[26:32, :] = jnp.zeros((6, LANES), jnp.float32)

    def pay_copy(d):
        rows = pl.ds(0, 32 if d == 1 else 24)
        return pltpu.make_async_remote_copy(
            src_ref=pay.at[rows],
            dst_ref=inbox.at[d - 1, rows],
            send_sem=pay_send.at[d - 1],
            recv_sem=pay_recv.at[d - 1],
            device_id={"ctx": lax.rem(c + d, ctx)},
            device_id_type=MESH,
        )

    for d in range(1, ctx):
        @pl.when(c + d < ctx)
        def _(d=d):
            pay_copy(d).start()

    query[...] = features(0, 0, ROWS)
    for r in range(8):
        shifted[r] = source[HALO - r : HALO - r + ROWS, :]
    inner[...] = jnp.zeros_like(inner)

    @pl.loop(0, 8)
    def _(r):
        for half in range(LANES // 128):
            lanes = slice(half * 128, half * 128 + 128)
            late_rows = [shifted[r, 8 * i : 8 * i + 8, lanes] for i in range(ROWS // 8)]
            sums = [inner[8 * i : 8 * i + 8, lanes] for i in range(ROWS // 8)]
            for q in range(ROWS // 8):
                tap = kern_rows[r, q, :, lanes]
                for i in range(q, ROWS // 8):
                    sums[i] = sums[i] + tap * late_rows[i - q]
            for i in range(ROWS // 8):
                inner[8 * i : 8 * i + 8, lanes] = sums[i]

    rates = decay[...]
    over = jnp.exp(-rates * ROWS)
    from_first = jnp.exp(-rates * (ROWS - 1.0))
    from_second = jnp.exp(-rates * (ROWS - 2.0))

    for d in range(1, ctx):
        @pl.when(c - d >= 0)
        def _(d=d):
            pay_copy(d).wait_recv()

    def lead(d, s):
        base = 16 + 4 * (s - 1)
        first = inbox[d - 1, base : base + 1, :]
        second = inbox[d - 1, base + 1 : base + 2, :]
        if d < ctx - 1:
            before = inbox[d, base + 2 : base + 3, :]
            last = inbox[d, base + 3 : base + 4, :]
        else:
            before = last = jnp.zeros((1, LANES), jnp.float32)
        t0, t1, t2 = (taps[j, s : s + 1, :] for j in range(3))
        return t0 * first + t1 * last + t2 * before, t0 * second + t1 * first + t2 * last

    state = jnp.zeros((MODES, LANES), jnp.float32)
    for d in range(ctx - 1, 0, -1):
        key_first, key_second = lead(d, 1)
        value_first, value_second = lead(d, 2)
        left = inbox[d - 1, 0:MODES, :]
        left = left + from_first * (key_first * value_first) + from_second * (key_second * value_second)
        state = over * state + left

    proj[0, HALO - 2 : HALO, :] = inbox[0, 24:26, :]
    proj[1, HALO - 2 : HALO, :] = inbox[0, 18:20, :]
    proj[2, HALO - 2 : HALO, :] = inbox[0, 22:24, :]
    query[0:8, :] = features(0, 0, 8)
    early = features(1, 0, 8) * features(2, 0, 8)

    response = inner[...]
    response = response + kern[HALO:, :] * early[0:1, :] + kern[HALO - 1 : HALO - 1 + ROWS, :] * early[1:2, :]
    for n in range(MODES):
        response = response + read[n] * state[n : n + 1, :]
    out[...] = (query[...] * response).astype(out.dtype)

    for d in range(1, ctx):
        @pl.when(c + d < ctx)
        def _(d=d):
            pay_copy(d).wait_send()
    sent = buf.at[pl.ds(0, count - 1)]
    pltpu.make_async_copy(sent, sent, send_sem.at[0]).wait()


def recv_count():
    passed = {p[:3] for p in PLAN if len(p) == 5 and p[1:3] != (0, 0)}
    return len(passed) + WIDE * DEEP


def on_device(tokens, in_weight, filter_taps, decay_rate, residue):
    count = lax.axis_size("tp")
    ctx = lax.axis_size("ctx")
    assert count == WIDE * DEEP
    weight = jnp.transpose(in_weight, (1, 0, 2))
    hbm = pl.BlockSpec(memory_space=pltpu.MemorySpace.HBM)
    f32 = jnp.float32
    scratch = [
        pltpu.VMEM((count, ROWS, LANES), jnp.bfloat16),
        pltpu.VMEM((count, 3, LANES, LANES), jnp.bfloat16),
        pltpu.VMEM((3, ROWS, LANES), f32),
        pltpu.VMEM((3, 3, LANES), f32),
        pltpu.VMEM((MODES, LANES), f32),
        pltpu.VMEM((MODES, LANES), f32),
        pltpu.VMEM((MODES, ROWS, LANES), f32),
        pltpu.VMEM((MODES, ROWS, LANES), f32),
        pltpu.VMEM((HALO + ROWS, LANES), f32),
        pltpu.VMEM((8, ROWS // 8, 8, LANES), f32),
        pltpu.VMEM((3, HALO + ROWS, LANES), f32),
        pltpu.VMEM((HALO + ROWS, LANES), f32),
        pltpu.VMEM((8, ROWS, LANES), f32),
        pltpu.VMEM((ROWS, LANES), f32),
        pltpu.VMEM((ROWS, LANES), f32),
        pltpu.VMEM((32, LANES), f32),
        pltpu.VMEM((ctx - 1, 32, LANES), f32),
        pltpu.SemaphoreType.DMA((4,)),
        pltpu.SemaphoreType.DMA((count // GROUP,)),
        pltpu.SemaphoreType.DMA((1,)),
        pltpu.SemaphoreType.DMA((recv_count(),)),
        pltpu.SemaphoreType.DMA((ctx - 1,)),
        pltpu.SemaphoreType.DMA((ctx - 1,)),
    ]

    def kernel(*refs):
        body(*refs)

    return pl.pallas_call(
        kernel,
        out_shape=jax.ShapeDtypeStruct((ROWS, LANES), jnp.bfloat16),
        in_specs=[hbm] * 5,
        out_specs=pl.BlockSpec(memory_space=pltpu.MemorySpace.VMEM),
        scratch_shapes=scratch,
        compiler_params=pltpu.CompilerParams(
            collective_id=0, has_side_effects=True, vmem_limit_bytes=56 * 1024 * 1024
        ),
        name="hyena",
    )(tokens, weight, filter_taps, decay_rate, residue)


def solution(mesh):
    return jax.shard_map(
        on_device,
        mesh=mesh,
        in_specs=(
            P("ctx", "tp"),
            P(None, None, "tp"),
            P(None, None, "tp"),
            P(None, "tp"),
            P(None, "tp"),
        ),
        out_specs=P("ctx", "tp"),
        check_vma=False,
    )
```

```python
import jax
import jax.numpy as jnp
from jax import lax
from jax.experimental import pallas as pl
from jax.experimental.pallas import tpu as pltpu
from jax.sharding import PartitionSpec as P

MESH = pl.DeviceIdType.MESH
PIECES = 2
PLAN = (
    (1, 0, 0, 1, 0), (0, 0, 0, 0, -1), (0, 0, 0, 0, 1), (0, 0, 0, -1, 0), (0, 0), (1, 0, 0, -1, 0), (1, 0, 0, 0, 1),
    (1, 0, 0, 0, -1), (0, 0, 0, 1, 0), (1, 0, 0, 0, -2), (0, 0, 0, 0, 2), (0, 3, 0, 0, -1), (0, 0, 1, -1, 0),
    (0, 0, 7, 1, 0), (1, 1, 0, 0, 1), (0, 0, 7, 0, -1), (1, 0, 7, 1, 0), (1, 0, 7, -1, 0), (1, 3, 0, 0, 1), (0, 1),
    (0, 7), (1, 0), (3, 0), (0, 1, 0, 0, 1), (0, 1, 0, 1, 0), (1, 3, 0, -1, 0), (1, 0, 6, 0, -1), (1, 0, 6, -1, 0),
    (0, 0, 2, 0, 1), (1, 0, 6, 1, 0), (1, 0, 6, 0, -2), (0, 0, 2, 1, 0), (0, 0, 2, -1, 0), (1, 1, 1, 0, 1),
    (1, 1, 1, 1, 0), (0, 3, 7, -1, 0), (1, 3, 1, 0, 1), (0, 0, 6, 0, -1), (1, 3, 7, -1, 0), (0, 0, 6, 1, 0), (0, 6),
    (1, 7), (3, 1), (3, 7), (0, 3, 7, 0, -1), (0, 2, 0, 0, 1), (1, 1), (2, 0), (1, 0, 5, -1, 0), (1, 0, 5, 1, 0),
    (0, 0, 3, 0, 1), (0, 0, 3, -1, 0), (1, 3, 6, 0, -2), (0, 0, 3, 1, 0), (0, 1, 2, 0, 2), (0, 3, 2, -1, 0),
    (1, 1, 2, 1, 0), (1, 2), (1, 0, 4, 1, 0), (0, 2, 7, 0, -1), (1, 3, 2, 0, 1), (3, 2), (0, 0, 5, -1, 0), (0, 5),
    (0, 0, 5, 1, 0), (1, 2, 7, 0, -1), (1, 6), (2, 7), (1, 1, 2, 0, 1), (1, 0, 4, 0, -1), (2, 1), (3, 6),
    (1, 3, 2, 1, 0), (1, 3, 5, -1, 0), (0, 2, 7, 0, -2), (0, 4), (0, 3, 3, 0, 1), (0, 3, 3, -1, 0), (1, 3, 4, -1, 0),
    (0, 1, 4, 1, 0), (1, 2, 2, 0, 1), (2, 2), (1, 4), (3, 5), (3, 3), (2, 6), (1, 5), (1, 3), (0, 3), (0, 2), (3, 4),
    (2, 5), (2, 3), (2, 4),
)
AHEAD = 12
FIRST_TABLE = 2
LANES = 256
ROWS = 128
MODES = 16
HALO = 8


WIDE, DEEP = 4, 8
GROUP = 4


def body(tokens, weight, taps_hbm, decay_hbm, residue_hbm, out, buf, wbuf, acc, taps, decay, residue,
         reversed_fall, read, kern, kern_rows, proj, source, shifted, inner, query, pay, inbox, rim, rim_in, query_rim, query_in,
         local_sem, weight_sem, send_sem, recv_sem, pay_send, pay_recv):
    count = WIDE * DEEP
    ctx = lax.axis_size("ctx")
    me = lax.axis_index("tp")
    c = lax.axis_index("ctx")
    my, mz = me // DEEP, lax.rem(me, DEEP)
    sends = [p for p in PLAN if len(p) == 5]
    blocks = [p for p in PLAN if len(p) == 2]
    piece = ROWS // PIECES
    turn = 1

    def at_offset(dy, dz):
        return lax.rem(my + turn * dy + 2 * WIDE, WIDE) * DEEP + lax.rem(mz + turn * dz + 2 * DEEP, DEEP)

    steps = sorted({p[3:] for p in sends})
    slots = {v: i for i, v in enumerate(blocks)}

    def slot(v):
        return slots[v]

    def weight_copy(v):
        rows = pl.ds(pl.multiple_of(at_offset(-v[0], -v[1]) * LANES, LANES), LANES)
        return pltpu.make_async_copy(weight.at[:, rows, :], wbuf.at[slot(v)], weight_sem.at[slot(v) // GROUP])

    def weight_wait(group):
        some = wbuf.at[pl.ds(group * GROUP, GROUP)]
        pltpu.make_async_copy(some, some, weight_sem.at[group]).wait()

    own = pltpu.make_async_copy(tokens, buf.at[0], local_sem.at[0])
    small = [
        pltpu.make_async_copy(taps_hbm, taps, local_sem.at[1]),
        pltpu.make_async_copy(decay_hbm, decay, local_sem.at[2]),
        pltpu.make_async_copy(residue_hbm, residue, local_sem.at[3]),
    ]

    barrier = pltpu.get_barrier_semaphore()
    for dy, dz in steps:
        pl.semaphore_signal(barrier, inc=1, device_id={"tp": at_offset(-dy, -dz)}, device_id_type=MESH)
    inbox[...] = jnp.zeros_like(inbox)
    rim_in[...] = jnp.zeros_like(rim_in)
    query_in[...] = jnp.zeros_like(query_in)
    query_rim[...] = jnp.zeros_like(query_rim)
    for d in range(1, ctx):
        @pl.when(c - d >= 0)
        def _(d=d):
            pl.semaphore_signal(barrier, inc=1, device_id={"ctx": c - d}, device_id_type=MESH)
    own.start()
    for copy in small:
        copy.start()
    for v in blocks[:AHEAD]:
        weight_copy(v).start()
    proj[:, 0:HALO, :] = jnp.zeros((3, HALO, LANES), jnp.float32)
    source[0:HALO, :] = jnp.zeros((HALO, LANES), jnp.float32)
    kern[...] = jnp.zeros_like(kern)
    pl.semaphore_wait(barrier, len(steps) + ctx - 1 - c)

    passed = {(h, (y, z)) for h, y, z, _, _ in sends}
    kept = sorted(p for p in passed if p[1] != (0, 0))
    order_of = {p: i for i, p in enumerate(kept)}
    leaves = {v: [h for h in range(PIECES) if (h, v) not in passed] for v in blocks}

    def recv_at(h, w):
        return recv_sem.at[order_of[h, w] if (h, w) in passed else len(kept) + slot(w)]

    def piece_copy(step, h, v, w):
        rows = pl.ds(h * piece, piece)
        src = tokens.at[rows] if v == (0, 0) else buf.at[slot(v), rows]
        return pltpu.make_async_remote_copy(
            src_ref=src,
            dst_ref=buf.at[slot(w), rows],
            send_sem=send_sem.at[0],
            recv_sem=recv_at(h, w),
            device_id={"tp": at_offset(*step)},
            device_id_type=MESH,
        )

    arrived = {(h, (0, 0)) for h in range(PIECES)}

    def await_piece(h, v):
        if (h, v) not in arrived:
            arrived.add((h, v))
            ref = buf.at[slot(v), pl.ds(h * piece, piece)]
            pltpu.make_async_copy(ref, ref, recv_at(h, v)).wait()

    def await_leaves(v):
        if leaves[v]:
            ref = buf.at[slot(v), pl.ds(0, piece * len(leaves[v]))]
            pltpu.make_async_copy(ref, ref, recv_at(leaves[v][0], v)).wait()

    def table(n):
        if n == 0:
            for copy in small:
                copy.wait()
        rate = decay[n : n + 1, :]
        coeff = residue[n : n + 1, :] * jnp.sqrt(1.0 - jnp.exp(-2.0 * rate))
        at = lax.broadcasted_iota(jnp.int32, (ROWS, LANES), 0).astype(jnp.float32)
        falling = jnp.exp(-rate * at)
        reversed_fall[n] = jnp.exp(-rate * (ROWS - 1.0 - at))
        read[n] = (coeff * jnp.exp(-rate)) * falling
        kern[HALO:, :] += coeff * falling

    def spread():
        @pl.loop(0, ROWS // 8)
        def _(q):
            rows = kern[pl.ds(pl.multiple_of(q * 8 + HALO, 8), 8), :]
            for r in range(8):
                kern_rows[r, q] = jnp.broadcast_to(rows[r : r + 1, :], (8, LANES))

    def multiply(order, v):
        if v == (0, 0):
            own.wait()
        for h in range(PIECES):
            if (h, v) in passed:
                await_piece(h, v)
        await_leaves(v)
        if order % GROUP == 0:
            weight_wait(order // GROUP)
        lhs = buf[slot(v)]
        for s in range(3):
            part = jnp.dot(lhs, wbuf[slot(v), s], preferred_element_type=jnp.float32)
            if order == 0:
                acc[s] = part
            else:
                acc[s] += part

    tables = 0
    for p in PLAN:
        if len(p) == 5:
            h, v, step = p[0], p[1:3], p[3:]
            w = (v[0] + step[0]) % WIDE, (v[1] + step[1]) % DEEP
            await_piece(h, v)
            piece_copy(step, h, v, w).start()
            continue
        i = slot(p)
        if i + AHEAD < count:
            weight_copy(blocks[i + AHEAD]).start()
        multiply(i, p)
        if tables < MODES and i >= FIRST_TABLE:
            table(tables)
            tables += 1
            if tables == MODES:
                spread()

    def features(s, first, rows):
        at = first + HALO
        total = taps[0, s : s + 1, :] * proj[s, at : at + rows, :]
        total = total + taps[1, s : s + 1, :] * proj[s, at - 1 : at - 1 + rows, :]
        return total + taps[2, s : s + 1, :] * proj[s, at - 2 : at - 2 + rows, :]

    def project(s):
        rounded = acc[s].astype(jnp.bfloat16)
        proj[s, HALO:, :] = rounded.astype(jnp.float32)
        return rounded

    def copy_to(d, src, dst, index):
        return pltpu.make_async_remote_copy(
            src_ref=src,
            dst_ref=dst,
            send_sem=pay_send.at[index],
            recv_sem=pay_recv.at[index],
            device_id={"ctx": lax.rem(c + d, ctx)},
            device_id_type=MESH,
        )

    def rim_copy(d):
        return copy_to(d, rim, rim_in.at[d - 1], d - 1)

    def pay_copy(d):
        return copy_to(d, pay, inbox.at[d - 1], ctx - 1 + d - 1)

    def query_copy():
        return copy_to(1, query_rim, query_in, 2 * (ctx - 1))

    def to_later(act):
        for d in range(1, ctx):
            @pl.when(c + d < ctx)
            def _(d=d):
                act(d)

    def from_earlier(act):
        for d in range(1, ctx):
            @pl.when(c - d >= 0)
            def _(d=d):
                act(d)

    key, value = project(1), project(2)
    rim[...] = jnp.concatenate([key[0:2], key[ROWS - 2 :], value[0:2], value[ROWS - 2 :]], axis=0)
    to_later(lambda d: rim_copy(d).start())
    rows_in = lax.broadcasted_iota(jnp.int32, (ROWS, LANES), 0)
    late = jnp.where(rows_in >= 2, features(1, 0, ROWS) * features(2, 0, ROWS), 0.0)
    source[HALO:, :] = late
    for n in range(MODES):
        pay[n : n + 1, :] = jnp.sum(reversed_fall[n] * late, axis=0, keepdims=True)
    to_later(lambda d: pay_copy(d).start())
    query_rim[0:2, :] = project(0)[ROWS - 2 :]

    @pl.when(c + 1 < ctx)
    def _():
        query_copy().start()

    query[...] = features(0, 0, ROWS)
    for r in range(8):
        shifted[r] = source[HALO - r : HALO - r + ROWS, :]
    inner[...] = jnp.zeros_like(inner)

    @pl.loop(0, 8)
    def _(r):
        for half in range(LANES // 128):
            lanes = slice(half * 128, half * 128 + 128)
            late_rows = [shifted[r, 8 * i : 8 * i + 8, lanes] for i in range(ROWS // 8)]
            sums = [inner[8 * i : 8 * i + 8, lanes] for i in range(ROWS // 8)]
            for q in range(ROWS // 8):
                tap = kern_rows[r, q, :, lanes]
                for i in range(q, ROWS // 8):
                    sums[i] = sums[i] + tap * late_rows[i - q]
            for i in range(ROWS // 8):
                inner[8 * i : 8 * i + 8, lanes] = sums[i]

    rates = decay[...]
    over = jnp.exp(-rates * ROWS)
    from_first = jnp.exp(-rates * (ROWS - 1.0))
    from_second = jnp.exp(-rates * (ROWS - 2.0))

    from_earlier(lambda d: rim_copy(d).wait_recv())
    rims = [rim_in[d].astype(jnp.float32) for d in range(ctx - 1)]

    def lead(d, s):
        base = 4 * (s - 1)
        first, second = rims[d - 1][base : base + 1], rims[d - 1][base + 1 : base + 2]
        if d < ctx - 1:
            before, last = rims[d][base + 2 : base + 3], rims[d][base + 3 : base + 4]
        else:
            before = last = jnp.zeros((1, LANES), jnp.float32)
        t0, t1, t2 = (taps[j, s : s + 1, :] for j in range(3))
        return t0 * first + t1 * last + t2 * before, t0 * second + t1 * first + t2 * last

    state = jnp.zeros((MODES, LANES), jnp.float32)
    for d in range(ctx - 1, 0, -1):
        key_first, key_second = lead(d, 1)
        value_first, value_second = lead(d, 2)
        left = from_first * (key_first * value_first) + from_second * (key_second * value_second)
        state = over * state + left

    proj[1, HALO - 2 : HALO, :] = rims[0][2:4]
    proj[2, HALO - 2 : HALO, :] = rims[0][6:8]
    early = features(1, 0, 8) * features(2, 0, 8)
    inner[...] += kern[HALO:, :] * early[0:1, :] + kern[HALO - 1 : HALO - 1 + ROWS, :] * early[1:2, :]

    @pl.when(c > 0)
    def _():
        query_copy().wait_recv()

    proj[0, HALO - 2 : HALO, :] = query_in[0:2, :].astype(jnp.float32)
    query[0:8, :] = features(0, 0, 8)

    from_earlier(lambda d: pay_copy(d).wait_recv())
    others = jnp.zeros((MODES, LANES), jnp.float32)
    for d in range(ctx - 1, 0, -1):
        others = over * others + inbox[d - 1]
    state = state + others

    response = inner[...]
    for n in range(MODES):
        response = response + read[n] * state[n : n + 1, :]
    out[...] = (query[...] * response).astype(out.dtype)

    to_later(lambda d: rim_copy(d).wait_send())
    to_later(lambda d: pay_copy(d).wait_send())

    @pl.when(c + 1 < ctx)
    def _():
        query_copy().wait_send()

    sent = buf.at[pl.ds(0, count - 1)]
    pltpu.make_async_copy(sent, sent, send_sem.at[0]).wait()


def recv_count():
    passed = {p[:3] for p in PLAN if len(p) == 5 and p[1:3] != (0, 0)}
    return len(passed) + WIDE * DEEP


def on_device(tokens, in_weight, filter_taps, decay_rate, residue):
    count = lax.axis_size("tp")
    ctx = lax.axis_size("ctx")
    assert count == WIDE * DEEP
    operands = (tokens, jnp.transpose(in_weight, (1, 0, 2)), filter_taps, decay_rate, residue)
    hbm = pl.BlockSpec(memory_space=pltpu.MemorySpace.HBM)
    f32 = jnp.float32
    scratch = [
        pltpu.VMEM((count, ROWS, LANES), jnp.bfloat16),
        pltpu.VMEM((count, 3, LANES, LANES), jnp.bfloat16),
        pltpu.VMEM((3, ROWS, LANES), f32),
        pltpu.VMEM((3, 3, LANES), f32),
        pltpu.VMEM((MODES, LANES), f32),
        pltpu.VMEM((MODES, LANES), f32),
        pltpu.VMEM((MODES, ROWS, LANES), f32),
        pltpu.VMEM((MODES, ROWS, LANES), f32),
        pltpu.VMEM((HALO + ROWS, LANES), f32),
        pltpu.VMEM((8, ROWS // 8, 8, LANES), f32),
        pltpu.VMEM((3, HALO + ROWS, LANES), f32),
        pltpu.VMEM((HALO + ROWS, LANES), f32),
        pltpu.VMEM((8, ROWS, LANES), f32),
        pltpu.VMEM((ROWS, LANES), f32),
        pltpu.VMEM((ROWS, LANES), f32),
        pltpu.VMEM((MODES, LANES), f32),
        pltpu.VMEM((ctx - 1, MODES, LANES), f32),
        pltpu.VMEM((8, LANES), jnp.bfloat16),
        pltpu.VMEM((ctx - 1, 8, LANES), jnp.bfloat16),
        pltpu.VMEM((8, LANES), jnp.bfloat16),
        pltpu.VMEM((8, LANES), jnp.bfloat16),
        pltpu.SemaphoreType.DMA((4,)),
        pltpu.SemaphoreType.DMA((count // GROUP,)),
        pltpu.SemaphoreType.DMA((1,)),
        pltpu.SemaphoreType.DMA((recv_count(),)),
        pltpu.SemaphoreType.DMA((2 * ctx - 1,)),
        pltpu.SemaphoreType.DMA((2 * ctx - 1,)),
    ]

    def kernel(*refs):
        body(*refs)

    return pl.pallas_call(
        kernel,
        out_shape=jax.ShapeDtypeStruct((ROWS, LANES), jnp.bfloat16),
        in_specs=[hbm] * 5,
        out_specs=pl.BlockSpec(memory_space=pltpu.MemorySpace.VMEM),
        scratch_shapes=scratch,
        compiler_params=pltpu.CompilerParams(
            collective_id=0, has_side_effects=True, vmem_limit_bytes=48 * 1024 * 1024
        ),
        name="hyena",
    )(*(pltpu.with_memory_space_constraint(a, pltpu.MemorySpace.HBM) for a in operands))


def solution(mesh):
    return jax.shard_map(
        on_device,
        mesh=mesh,
        in_specs=(
            P("ctx", "tp"),
            P(None, None, "tp"),
            P(None, None, "tp"),
            P(None, "tp"),
            P(None, "tp"),
        ),
        out_specs=P("ctx", "tp"),
        check_vma=False,
    )
```

```python
import jax
import jax.numpy as jnp
from jax import lax
from jax.experimental import pallas as pl
from jax.experimental.pallas import tpu as pltpu
from jax.sharding import PartitionSpec as P

MESH = pl.DeviceIdType.MESH
PIECES = 2
PLAN = (
    (1, 0, 0, -1, 0), (1, 0, 0, 0, 1), (0, 0, 0, 0, -1), (0, 0), (1, 0, 0, 0, -1), (1, 0, 0, 1, 0), (0, 0, 0, 0, 1),
    (0, 0, 0, 0, 2), (0, 0, 0, 1, 0), (1, 0, 0, 0, -2), (0, 0, 0, -1, 0), (1, 0, 1, -1, 0), (0, 0, 7, 1, 0),
    (1, 3, 0, 0, -1), (1, 0, 1, 0, 1), (0, 3, 0, 0, 1), (1, 0, 7, 1, 0), (0, 3, 0, -1, 0), (0, 3, 0, 0, -1), (0, 1),
    (0, 7), (1, 0), (3, 0), (1, 1, 0, 0, 1), (0, 0, 1, 1, 0), (0, 0, 7, 0, -1), (1, 3, 0, -1, 0), (1, 0, 6, 0, -1),
    (1, 0, 6, 1, 0), (0, 0, 2, -1, 0), (0, 0, 2, 0, 1), (1, 0, 6, -1, 0), (0, 0, 2, 1, 0), (0, 0, 2, 0, 2),
    (1, 0, 6, 0, -2), (1, 0, 2, -1, 0), (0, 1, 7, 1, 0), (0, 2), (1, 0, 2, 0, 1), (1, 0, 2, 1, 0), (0, 1, 7, 0, -1),
    (0, 3, 1, -1, 0), (1, 7), (3, 1), (3, 7), (1, 1, 7, 1, 0), (0, 0, 6, 0, -1), (1, 2, 0, 0, 1), (0, 0, 6, -1, 0),
    (1, 1), (2, 0), (0, 3, 2, 0, 1), (1, 0, 5, 1, 0), (1, 0, 5, -1, 0), (1, 1, 6, 0, -2), (0, 6), (0, 1, 2, 0, 1),
    (0, 0, 4, 1, 0), (0, 0, 4, -1, 0), (0, 4), (1, 0, 4, -1, 0), (0, 1, 2, 1, 0), (1, 3, 2, 0, 1), (0, 2, 7, 0, -1),
    (1, 1, 6, 1, 0), (1, 3, 2, -1, 0), (1, 1, 2, 0, 1), (3, 2), (0, 1, 6, 0, -1), (0, 3), (1, 2), (1, 6),
    (0, 3, 6, 0, -1), (1, 2, 1, 0, 2), (0, 5), (2, 1), (2, 7), (3, 6), (0, 2, 7, 0, -2), (1, 1, 5, 1, 0),
    (0, 3, 3, -1, 0), (1, 1, 4, 1, 0), (0, 3, 4, -1, 0), (1, 4), (3, 3), (3, 4), (1, 3), (1, 5), (2, 2), (2, 6),
    (3, 5), (2, 3), (2, 4), (2, 5),
)
AHEAD = 16
FIRST_TABLE = 2
LANES = 256
ROWS = 128
MODES = 16
HALO = 8


WIDE, DEEP = 4, 8
GROUP = 4


def body(tokens, weight, taps_hbm, decay_hbm, residue_hbm, out, buf, wbuf, acc, taps, decay, residue,
         reversed_fall, read, kern, kern_rows, proj, source, shifted, inner, query, pay, inbox, rim, rim_in, query_rim, query_in,
         local_sem, weight_sem, send_sem, recv_sem, pay_send, pay_recv):
    count = WIDE * DEEP
    ctx = lax.axis_size("ctx")
    me = lax.axis_index("tp")
    c = lax.axis_index("ctx")
    my, mz = me // DEEP, lax.rem(me, DEEP)
    sends = [p for p in PLAN if len(p) == 5]
    blocks = [p for p in PLAN if len(p) == 2]
    piece = ROWS // PIECES
    turn = 1

    def at_offset(dy, dz):
        return lax.rem(my + turn * dy + 2 * WIDE, WIDE) * DEEP + lax.rem(mz + turn * dz + 2 * DEEP, DEEP)

    steps = sorted({p[3:] for p in sends})
    slots = {v: i for i, v in enumerate(blocks)}

    def slot(v):
        return slots[v]

    def weight_copy(v):
        rows = pl.ds(pl.multiple_of(at_offset(-v[0], -v[1]) * LANES, LANES), LANES)
        return pltpu.make_async_copy(weight.at[:, rows, :], wbuf.at[slot(v)], weight_sem.at[slot(v) // GROUP])

    def weight_wait(group):
        some = wbuf.at[pl.ds(group * GROUP, GROUP)]
        pltpu.make_async_copy(some, some, weight_sem.at[group]).wait()

    own = pltpu.make_async_copy(tokens, buf.at[0], local_sem.at[0])
    small = [
        pltpu.make_async_copy(taps_hbm, taps, local_sem.at[1]),
        pltpu.make_async_copy(decay_hbm, decay, local_sem.at[2]),
        pltpu.make_async_copy(residue_hbm, residue, local_sem.at[3]),
    ]

    barrier = pltpu.get_barrier_semaphore()
    for dy, dz in steps:
        pl.semaphore_signal(barrier, inc=1, device_id={"tp": at_offset(-dy, -dz)}, device_id_type=MESH)
    inbox[...] = jnp.zeros_like(inbox)
    rim_in[...] = jnp.zeros_like(rim_in)
    query_in[...] = jnp.zeros_like(query_in)
    query_rim[...] = jnp.zeros_like(query_rim)
    for d in range(1, ctx):
        @pl.when(c - d >= 0)
        def _(d=d):
            pl.semaphore_signal(barrier, inc=1, device_id={"ctx": c - d}, device_id_type=MESH)
    own.start()
    for copy in small:
        copy.start()
    for v in blocks[:AHEAD]:
        weight_copy(v).start()
    proj[:, 0:HALO, :] = jnp.zeros((3, HALO, LANES), jnp.float32)
    source[0:HALO, :] = jnp.zeros((HALO, LANES), jnp.float32)
    kern[...] = jnp.zeros_like(kern)
    own.wait()
    pl.semaphore_wait(barrier, len(steps) + ctx - 1 - c)

    passed = {(h, (y, z)) for h, y, z, _, _ in sends}
    kept = sorted(p for p in passed if p[1] != (0, 0))
    order_of = {p: i for i, p in enumerate(kept)}
    leaves = {v: [h for h in range(PIECES) if (h, v) not in passed] for v in blocks}

    def recv_at(h, w):
        return recv_sem.at[order_of[h, w] if (h, w) in passed else len(kept) + slot(w)]

    def piece_copy(step, h, v, w):
        rows = pl.ds(h * piece, piece)
        return pltpu.make_async_remote_copy(
            src_ref=buf.at[slot(v), rows],
            dst_ref=buf.at[slot(w), rows],
            send_sem=send_sem.at[0],
            recv_sem=recv_at(h, w),
            device_id={"tp": at_offset(*step)},
            device_id_type=MESH,
        )

    arrived = {(h, (0, 0)) for h in range(PIECES)}

    def await_piece(h, v):
        if (h, v) not in arrived:
            arrived.add((h, v))
            ref = buf.at[slot(v), pl.ds(h * piece, piece)]
            pltpu.make_async_copy(ref, ref, recv_at(h, v)).wait()

    def await_leaves(v):
        if leaves[v]:
            ref = buf.at[slot(v), pl.ds(0, piece * len(leaves[v]))]
            pltpu.make_async_copy(ref, ref, recv_at(leaves[v][0], v)).wait()

    def table(n):
        if n == 0:
            for copy in small:
                copy.wait()
        rate = decay[n : n + 1, :]
        coeff = residue[n : n + 1, :] * jnp.sqrt(1.0 - jnp.exp(-2.0 * rate))
        at = lax.broadcasted_iota(jnp.int32, (ROWS, LANES), 0).astype(jnp.float32)
        falling = jnp.exp(-rate * at)
        reversed_fall[n] = jnp.exp(-rate * (ROWS - 1.0 - at))
        read[n] = (coeff * jnp.exp(-rate)) * falling
        kern[HALO:, :] += coeff * falling

    def spread():
        @pl.loop(0, ROWS // 8)
        def _(q):
            rows = kern[pl.ds(pl.multiple_of(q * 8 + HALO, 8), 8), :]
            for r in range(8):
                kern_rows[r, q] = jnp.broadcast_to(rows[r : r + 1, :], (8, LANES))

    def multiply(order, v):
        for h in range(PIECES):
            if (h, v) in passed:
                await_piece(h, v)
        await_leaves(v)
        if order % GROUP == 0:
            weight_wait(order // GROUP)
        lhs = buf[slot(v)]
        for s in range(3):
            part = jnp.dot(lhs, wbuf[slot(v), s], preferred_element_type=jnp.float32)
            if order == 0:
                acc[s] = part
            else:
                acc[s] += part

    tables = 0
    for p in PLAN:
        if len(p) == 5:
            h, v, step = p[0], p[1:3], p[3:]
            w = (v[0] + step[0]) % WIDE, (v[1] + step[1]) % DEEP
            await_piece(h, v)
            piece_copy(step, h, v, w).start()
            continue
        i = slot(p)
        if i + AHEAD < count:
            weight_copy(blocks[i + AHEAD]).start()
        multiply(i, p)
        if tables < MODES and i >= FIRST_TABLE:
            table(tables)
            tables += 1
            if tables == MODES:
                spread()

    def features(s, first, rows):
        at = first + HALO
        total = taps[0, s : s + 1, :] * proj[s, at : at + rows, :]
        total = total + taps[1, s : s + 1, :] * proj[s, at - 1 : at - 1 + rows, :]
        return total + taps[2, s : s + 1, :] * proj[s, at - 2 : at - 2 + rows, :]

    def project(s):
        rounded = acc[s].astype(jnp.bfloat16)
        proj[s, HALO:, :] = rounded.astype(jnp.float32)
        return rounded

    def copy_to(d, src, dst, index):
        return pltpu.make_async_remote_copy(
            src_ref=src,
            dst_ref=dst,
            send_sem=pay_send.at[index],
            recv_sem=pay_recv.at[index],
            device_id={"ctx": lax.rem(c + d, ctx)},
            device_id_type=MESH,
        )

    def rim_copy(d):
        return copy_to(d, rim, rim_in.at[d - 1], d - 1)

    def pay_copy(d):
        return copy_to(d, pay, inbox.at[d - 1], ctx - 1 + d - 1)

    def query_copy():
        return copy_to(1, query_rim, query_in, 2 * (ctx - 1))

    def to_later(act):
        for d in range(1, ctx):
            @pl.when(c + d < ctx)
            def _(d=d):
                act(d)

    def from_earlier(act):
        for d in range(1, ctx):
            @pl.when(c - d >= 0)
            def _(d=d):
                act(d)

    key, value = project(1), project(2)
    rim[...] = jnp.concatenate([key[0:2], key[ROWS - 2 :], value[0:2], value[ROWS - 2 :]], axis=0)
    to_later(lambda d: rim_copy(d).start())
    rows_in = lax.broadcasted_iota(jnp.int32, (ROWS, LANES), 0)
    late = jnp.where(rows_in >= 2, features(1, 0, ROWS) * features(2, 0, ROWS), 0.0)
    source[HALO:, :] = late
    for n in range(MODES):
        pay[n : n + 1, :] = jnp.sum(reversed_fall[n] * late, axis=0, keepdims=True)
    to_later(lambda d: pay_copy(d).start())
    query_rim[0:2, :] = project(0)[ROWS - 2 :]

    @pl.when(c + 1 < ctx)
    def _():
        query_copy().start()

    query[...] = features(0, 0, ROWS)
    for r in range(8):
        shifted[r] = source[HALO - r : HALO - r + ROWS, :]
    inner[...] = jnp.zeros_like(inner)

    @pl.loop(0, 8)
    def _(r):
        for half in range(LANES // 128):
            lanes = slice(half * 128, half * 128 + 128)
            late_rows = [shifted[r, 8 * i : 8 * i + 8, lanes] for i in range(ROWS // 8)]
            sums = [inner[8 * i : 8 * i + 8, lanes] for i in range(ROWS // 8)]
            for q in range(ROWS // 8):
                tap = kern_rows[r, q, :, lanes]
                for i in range(q, ROWS // 8):
                    sums[i] = sums[i] + tap * late_rows[i - q]
            for i in range(ROWS // 8):
                inner[8 * i : 8 * i + 8, lanes] = sums[i]

    rates = decay[...]
    over = jnp.exp(-rates * ROWS)
    from_first = jnp.exp(-rates * (ROWS - 1.0))
    from_second = jnp.exp(-rates * (ROWS - 2.0))

    from_earlier(lambda d: rim_copy(d).wait_recv())
    rims = [rim_in[d].astype(jnp.float32) for d in range(ctx - 1)]

    def lead(d, s):
        base = 4 * (s - 1)
        first, second = rims[d - 1][base : base + 1], rims[d - 1][base + 1 : base + 2]
        if d < ctx - 1:
            before, last = rims[d][base + 2 : base + 3], rims[d][base + 3 : base + 4]
        else:
            before = last = jnp.zeros((1, LANES), jnp.float32)
        t0, t1, t2 = (taps[j, s : s + 1, :] for j in range(3))
        return t0 * first + t1 * last + t2 * before, t0 * second + t1 * first + t2 * last

    state = jnp.zeros((MODES, LANES), jnp.float32)
    for d in range(ctx - 1, 0, -1):
        key_first, key_second = lead(d, 1)
        value_first, value_second = lead(d, 2)
        left = from_first * (key_first * value_first) + from_second * (key_second * value_second)
        state = over * state + left

    proj[1, HALO - 2 : HALO, :] = rims[0][2:4]
    proj[2, HALO - 2 : HALO, :] = rims[0][6:8]
    early = features(1, 0, 8) * features(2, 0, 8)
    inner[...] += kern[HALO:, :] * early[0:1, :] + kern[HALO - 1 : HALO - 1 + ROWS, :] * early[1:2, :]

    @pl.when(c > 0)
    def _():
        query_copy().wait_recv()

    proj[0, HALO - 2 : HALO, :] = query_in[0:2, :].astype(jnp.float32)
    query[0:8, :] = features(0, 0, 8)

    from_earlier(lambda d: pay_copy(d).wait_recv())
    others = jnp.zeros((MODES, LANES), jnp.float32)
    for d in range(ctx - 1, 0, -1):
        others = over * others + inbox[d - 1]
    state = state + others

    response = inner[...]
    for n in range(MODES):
        response = response + read[n] * state[n : n + 1, :]
    out[...] = (query[...] * response).astype(out.dtype)

    to_later(lambda d: rim_copy(d).wait_send())
    to_later(lambda d: pay_copy(d).wait_send())

    @pl.when(c + 1 < ctx)
    def _():
        query_copy().wait_send()

    sent = buf.at[pl.ds(0, count - 1)]
    pltpu.make_async_copy(sent, sent, send_sem.at[0]).wait()


def recv_count():
    passed = {p[:3] for p in PLAN if len(p) == 5 and p[1:3] != (0, 0)}
    return len(passed) + WIDE * DEEP


def on_device(tokens, in_weight, filter_taps, decay_rate, residue):
    count = lax.axis_size("tp")
    ctx = lax.axis_size("ctx")
    assert count == WIDE * DEEP
    operands = (tokens, jnp.transpose(in_weight, (1, 0, 2)), filter_taps, decay_rate, residue)
    hbm = pl.BlockSpec(memory_space=pltpu.MemorySpace.HBM)
    f32 = jnp.float32
    scratch = [
        pltpu.VMEM((count, ROWS, LANES), jnp.bfloat16),
        pltpu.VMEM((count, 3, LANES, LANES), jnp.bfloat16),
        pltpu.VMEM((3, ROWS, LANES), f32),
        pltpu.VMEM((3, 3, LANES), f32),
        pltpu.VMEM((MODES, LANES), f32),
        pltpu.VMEM((MODES, LANES), f32),
        pltpu.VMEM((MODES, ROWS, LANES), f32),
        pltpu.VMEM((MODES, ROWS, LANES), f32),
        pltpu.VMEM((HALO + ROWS, LANES), f32),
        pltpu.VMEM((8, ROWS // 8, 8, LANES), f32),
        pltpu.VMEM((3, HALO + ROWS, LANES), f32),
        pltpu.VMEM((HALO + ROWS, LANES), f32),
        pltpu.VMEM((8, ROWS, LANES), f32),
        pltpu.VMEM((ROWS, LANES), f32),
        pltpu.VMEM((ROWS, LANES), f32),
        pltpu.VMEM((MODES, LANES), f32),
        pltpu.VMEM((ctx - 1, MODES, LANES), f32),
        pltpu.VMEM((8, LANES), jnp.bfloat16),
        pltpu.VMEM((ctx - 1, 8, LANES), jnp.bfloat16),
        pltpu.VMEM((8, LANES), jnp.bfloat16),
        pltpu.VMEM((8, LANES), jnp.bfloat16),
        pltpu.SemaphoreType.DMA((4,)),
        pltpu.SemaphoreType.DMA((count // GROUP,)),
        pltpu.SemaphoreType.DMA((1,)),
        pltpu.SemaphoreType.DMA((recv_count(),)),
        pltpu.SemaphoreType.DMA((2 * ctx - 1,)),
        pltpu.SemaphoreType.DMA((2 * ctx - 1,)),
    ]

    def kernel(*refs):
        body(*refs)

    return pl.pallas_call(
        kernel,
        out_shape=jax.ShapeDtypeStruct((ROWS, LANES), jnp.bfloat16),
        in_specs=[hbm] * 5,
        out_specs=pl.BlockSpec(memory_space=pltpu.MemorySpace.VMEM),
        scratch_shapes=scratch,
        compiler_params=pltpu.CompilerParams(
            collective_id=0, has_side_effects=True, vmem_limit_bytes=48 * 1024 * 1024
        ),
        name="hyena",
    )(*(pltpu.with_memory_space_constraint(a, pltpu.MemorySpace.HBM) for a in operands))


def solution(mesh):
    return jax.shard_map(
        on_device,
        mesh=mesh,
        in_specs=(
            P("ctx", "tp"),
            P(None, None, "tp"),
            P(None, None, "tp"),
            P(None, "tp"),
            P(None, "tp"),
        ),
        out_specs=P("ctx", "tp"),
        check_vma=False,
    )
```

```python
import jax
import jax.numpy as jnp
from jax import lax
from jax.experimental import pallas as pl
from jax.experimental.pallas import tpu as pltpu
from jax.sharding import PartitionSpec as P

MESH = pl.DeviceIdType.MESH
PIECES = 2
PLAN = (
    (1, 0, 0, -1, 0), (1, 0, 0, 0, 1), (0, 0, 0, 0, -1), (0, 0), (1, 0, 0, 0, -1), (1, 0, 0, 1, 0), (0, 0, 0, 0, 1),
    (0, 0, 0, 0, 2), (0, 0, 0, 1, 0), (1, 0, 0, 0, -2), (0, 0, 0, -1, 0), (1, 0, 1, -1, 0), (0, 0, 7, 1, 0),
    (1, 3, 0, 0, -1), (1, 0, 1, 0, 1), (0, 3, 0, 0, 1), (1, 0, 7, 1, 0), (0, 3, 0, -1, 0), (0, 3, 0, 0, -1), (0, 1),
    (0, 7), (1, 0), (3, 0), (1, 1, 0, 0, 1), (0, 0, 1, 1, 0), (0, 0, 7, 0, -1), (1, 3, 0, -1, 0), (1, 0, 6, 0, -1),
    (1, 0, 6, 1, 0), (0, 0, 2, -1, 0), (0, 0, 2, 0, 1), (1, 0, 6, -1, 0), (0, 0, 2, 1, 0), (0, 0, 2, 0, 2),
    (1, 0, 6, 0, -2), (1, 0, 2, -1, 0), (0, 1, 7, 1, 0), (0, 2), (1, 0, 2, 0, 1), (1, 0, 2, 1, 0), (0, 1, 7, 0, -1),
    (0, 3, 1, -1, 0), (1, 7), (3, 1), (3, 7), (1, 1, 7, 1, 0), (0, 0, 6, 0, -1), (1, 2, 0, 0, 1), (0, 0, 6, -1, 0),
    (1, 1), (2, 0), (0, 3, 2, 0, 1), (1, 0, 5, 1, 0), (1, 0, 5, -1, 0), (1, 1, 6, 0, -2), (0, 6), (0, 1, 2, 0, 1),
    (0, 0, 4, 1, 0), (0, 0, 4, -1, 0), (0, 4), (1, 0, 4, -1, 0), (0, 1, 2, 1, 0), (1, 3, 2, 0, 1), (0, 2, 7, 0, -1),
    (1, 1, 6, 1, 0), (1, 3, 2, -1, 0), (1, 1, 2, 0, 1), (3, 2), (0, 1, 6, 0, -1), (0, 3), (1, 2), (1, 6),
    (0, 3, 6, 0, -1), (1, 2, 1, 0, 2), (0, 5), (2, 1), (2, 7), (3, 6), (0, 2, 7, 0, -2), (1, 1, 5, 1, 0),
    (0, 3, 3, -1, 0), (1, 1, 4, 1, 0), (0, 3, 4, -1, 0), (1, 4), (3, 3), (3, 4), (1, 3), (1, 5), (2, 2), (2, 6),
    (3, 5), (2, 3), (2, 4), (2, 5),
)
AHEAD = 16
FIRST_TABLE = 2
LANES = 256
ROWS = 128
MODES = 16
HALO = 8


WIDE, DEEP = 4, 8
GROUP = 4


def body(tokens, weight, taps_hbm, decay_hbm, residue_hbm, out, buf, wbuf, acc, taps, decay, residue,
         reversed_fall, read, kern, kern_rows, proj, source, shifted, inner, query, pay, inbox, rim, rim_in, query_rim, query_in,
         local_sem, weight_sem, send_sem, recv_sem, pay_send, pay_recv):
    count = WIDE * DEEP
    ctx = lax.axis_size("ctx")
    me = lax.axis_index("tp")
    c = lax.axis_index("ctx")
    my, mz = me // DEEP, lax.rem(me, DEEP)
    sends = [p for p in PLAN if len(p) == 5]
    blocks = [p for p in PLAN if len(p) == 2]
    piece = ROWS // PIECES
    turn = 1

    def at_offset(dy, dz):
        return lax.rem(my + turn * dy + 2 * WIDE, WIDE) * DEEP + lax.rem(mz + turn * dz + 2 * DEEP, DEEP)

    steps = sorted({p[3:] for p in sends})
    slots = {v: i for i, v in enumerate(blocks)}

    def slot(v):
        return slots[v]

    def weight_copy(v):
        rows = pl.ds(pl.multiple_of(at_offset(-v[0], -v[1]) * LANES, LANES), LANES)
        return pltpu.make_async_copy(weight.at[:, rows, :], wbuf.at[slot(v)], weight_sem.at[slot(v) // GROUP])

    def weight_wait(group):
        some = wbuf.at[pl.ds(group * GROUP, GROUP)]
        pltpu.make_async_copy(some, some, weight_sem.at[group]).wait()

    own = pltpu.make_async_copy(tokens, buf.at[0], local_sem.at[0])
    small = [
        pltpu.make_async_copy(taps_hbm, taps, local_sem.at[1]),
        pltpu.make_async_copy(decay_hbm, decay, local_sem.at[2]),
        pltpu.make_async_copy(residue_hbm, residue, local_sem.at[3]),
    ]

    barrier = pltpu.get_barrier_semaphore()
    for dy, dz in steps:
        pl.semaphore_signal(barrier, inc=1, device_id={"tp": at_offset(-dy, -dz)}, device_id_type=MESH)
    inbox[...] = jnp.zeros_like(inbox)
    rim_in[...] = jnp.zeros_like(rim_in)
    query_in[...] = jnp.zeros_like(query_in)
    query_rim[...] = jnp.zeros_like(query_rim)
    for d in range(1, ctx):
        @pl.when(c - d >= 0)
        def _(d=d):
            pl.semaphore_signal(barrier, inc=1, device_id={"ctx": c - d}, device_id_type=MESH)
    own.start()
    for copy in small:
        copy.start()
    for v in blocks[:AHEAD]:
        weight_copy(v).start()
    proj[:, 0:HALO, :] = jnp.zeros((3, HALO, LANES), jnp.float32)
    source[0:HALO, :] = jnp.zeros((HALO, LANES), jnp.float32)
    kern[...] = jnp.zeros_like(kern)
    own.wait()
    pl.semaphore_wait(barrier, len(steps) + ctx - 1 - c)

    passed = {(h, (y, z)) for h, y, z, _, _ in sends}
    kept = sorted(p for p in passed if p[1] != (0, 0))
    order_of = {p: i for i, p in enumerate(kept)}
    leaves = {v: [h for h in range(PIECES) if (h, v) not in passed] for v in blocks}

    def recv_at(h, w):
        return recv_sem.at[order_of[h, w] if (h, w) in passed else len(kept) + slot(w)]

    def piece_copy(step, h, v, w):
        rows = pl.ds(h * piece, piece)
        return pltpu.make_async_remote_copy(
            src_ref=buf.at[slot(v), rows],
            dst_ref=buf.at[slot(w), rows],
            send_sem=send_sem.at[0],
            recv_sem=recv_at(h, w),
            device_id={"tp": at_offset(*step)},
            device_id_type=MESH,
        )

    arrived = {(h, (0, 0)) for h in range(PIECES)}

    def await_piece(h, v):
        if (h, v) not in arrived:
            arrived.add((h, v))
            ref = buf.at[slot(v), pl.ds(h * piece, piece)]
            pltpu.make_async_copy(ref, ref, recv_at(h, v)).wait()

    def await_leaves(v):
        if leaves[v]:
            ref = buf.at[slot(v), pl.ds(0, piece * len(leaves[v]))]
            pltpu.make_async_copy(ref, ref, recv_at(leaves[v][0], v)).wait()

    def table(n):
        if n == 0:
            for copy in small:
                copy.wait()
        rate = decay[n : n + 1, :]
        coeff = residue[n : n + 1, :] * jnp.sqrt(1.0 - jnp.exp(-2.0 * rate))
        at = lax.broadcasted_iota(jnp.int32, (ROWS, LANES), 0).astype(jnp.float32)
        falling = jnp.exp(-rate * at)
        reversed_fall[n] = jnp.exp(-rate * (ROWS - 1.0 - at))
        read[n] = (coeff * jnp.exp(-rate)) * falling
        kern[HALO:, :] += coeff * falling

    def spread():
        @pl.loop(0, ROWS // 8)
        def _(q):
            rows = kern[pl.ds(pl.multiple_of(q * 8 + HALO, 8), 8), :]
            for r in range(8):
                kern_rows[r, q] = jnp.broadcast_to(rows[r : r + 1, :], (8, LANES))

    def multiply(order):
        pair = blocks[order - 1 : order + 1]
        for v in pair:
            for h in range(PIECES):
                if (h, v) in passed:
                    await_piece(h, v)
            await_leaves(v)
        if (order - 1) % GROUP == 0:
            weight_wait((order - 1) // GROUP)
        for s in range(3):
            part = sum(
                jnp.dot(buf[slot(v)], wbuf[slot(v), s], preferred_element_type=jnp.float32) for v in pair
            )
            if order == 1:
                acc[s] = part
            else:
                acc[s] += part

    tables = 0
    for p in PLAN:
        if len(p) == 5:
            h, v, step = p[0], p[1:3], p[3:]
            w = (v[0] + step[0]) % WIDE, (v[1] + step[1]) % DEEP
            await_piece(h, v)
            piece_copy(step, h, v, w).start()
            continue
        i = slot(p)
        if i + AHEAD < count:
            weight_copy(blocks[i + AHEAD]).start()
        if i % 2 == 1:
            multiply(i)
        if tables < MODES and i >= FIRST_TABLE:
            table(tables)
            tables += 1
            if tables == MODES:
                spread()

    def features(s, first, rows):
        at = first + HALO
        total = taps[0, s : s + 1, :] * proj[s, at : at + rows, :]
        total = total + taps[1, s : s + 1, :] * proj[s, at - 1 : at - 1 + rows, :]
        return total + taps[2, s : s + 1, :] * proj[s, at - 2 : at - 2 + rows, :]

    def project(s):
        rounded = acc[s].astype(jnp.bfloat16)
        proj[s, HALO:, :] = rounded.astype(jnp.float32)
        return rounded

    def copy_to(d, src, dst, index):
        return pltpu.make_async_remote_copy(
            src_ref=src,
            dst_ref=dst,
            send_sem=pay_send.at[index],
            recv_sem=pay_recv.at[index],
            device_id={"ctx": lax.rem(c + d, ctx)},
            device_id_type=MESH,
        )

    def rim_copy(d):
        return copy_to(d, rim, rim_in.at[d - 1], d - 1)

    def pay_copy(d):
        return copy_to(d, pay, inbox.at[d - 1], ctx - 1 + d - 1)

    def query_copy():
        return copy_to(1, query_rim, query_in, 2 * (ctx - 1))

    def to_later(act):
        for d in range(1, ctx):
            @pl.when(c + d < ctx)
            def _(d=d):
                act(d)

    def from_earlier(act):
        for d in range(1, ctx):
            @pl.when(c - d >= 0)
            def _(d=d):
                act(d)

    key, value = project(1), project(2)
    rim[...] = jnp.concatenate([key[0:2], key[ROWS - 2 :], value[0:2], value[ROWS - 2 :]], axis=0)
    to_later(lambda d: rim_copy(d).start())
    rows_in = lax.broadcasted_iota(jnp.int32, (ROWS, LANES), 0)
    late = jnp.where(rows_in >= 2, features(1, 0, ROWS) * features(2, 0, ROWS), 0.0)
    source[HALO:, :] = late
    for n in range(MODES):
        pay[n : n + 1, :] = jnp.sum(reversed_fall[n] * late, axis=0, keepdims=True)
    to_later(lambda d: pay_copy(d).start())
    query_rim[0:2, :] = project(0)[ROWS - 2 :]

    @pl.when(c + 1 < ctx)
    def _():
        query_copy().start()

    query[...] = features(0, 0, ROWS)
    for r in range(8):
        shifted[r] = source[HALO - r : HALO - r + ROWS, :]
    inner[...] = jnp.zeros_like(inner)

    @pl.loop(0, 8)
    def _(r):
        for half in range(LANES // 128):
            lanes = slice(half * 128, half * 128 + 128)
            late_rows = [shifted[r, 8 * i : 8 * i + 8, lanes] for i in range(ROWS // 8)]
            sums = [inner[8 * i : 8 * i + 8, lanes] for i in range(ROWS // 8)]
            for q in range(ROWS // 8):
                tap = kern_rows[r, q, :, lanes]
                for i in range(q, ROWS // 8):
                    sums[i] = sums[i] + tap * late_rows[i - q]
            for i in range(ROWS // 8):
                inner[8 * i : 8 * i + 8, lanes] = sums[i]

    rates = decay[...]
    over = jnp.exp(-rates * ROWS)
    from_first = jnp.exp(-rates * (ROWS - 1.0))
    from_second = jnp.exp(-rates * (ROWS - 2.0))

    from_earlier(lambda d: rim_copy(d).wait_recv())
    rims = [rim_in[d].astype(jnp.float32) for d in range(ctx - 1)]

    def lead(d, s):
        base = 4 * (s - 1)
        first, second = rims[d - 1][base : base + 1], rims[d - 1][base + 1 : base + 2]
        if d < ctx - 1:
            before, last = rims[d][base + 2 : base + 3], rims[d][base + 3 : base + 4]
        else:
            before = last = jnp.zeros((1, LANES), jnp.float32)
        t0, t1, t2 = (taps[j, s : s + 1, :] for j in range(3))
        return t0 * first + t1 * last + t2 * before, t0 * second + t1 * first + t2 * last

    state = jnp.zeros((MODES, LANES), jnp.float32)
    for d in range(ctx - 1, 0, -1):
        key_first, key_second = lead(d, 1)
        value_first, value_second = lead(d, 2)
        left = from_first * (key_first * value_first) + from_second * (key_second * value_second)
        state = over * state + left

    proj[1, HALO - 2 : HALO, :] = rims[0][2:4]
    proj[2, HALO - 2 : HALO, :] = rims[0][6:8]
    early = features(1, 0, 8) * features(2, 0, 8)
    inner[...] += kern[HALO:, :] * early[0:1, :] + kern[HALO - 1 : HALO - 1 + ROWS, :] * early[1:2, :]

    @pl.when(c > 0)
    def _():
        query_copy().wait_recv()

    proj[0, HALO - 2 : HALO, :] = query_in[0:2, :].astype(jnp.float32)
    query[0:8, :] = features(0, 0, 8)

    from_earlier(lambda d: pay_copy(d).wait_recv())
    others = jnp.zeros((MODES, LANES), jnp.float32)
    for d in range(ctx - 1, 0, -1):
        others = over * others + inbox[d - 1]
    state = state + others

    response = inner[...]
    for n in range(MODES):
        response = response + read[n] * state[n : n + 1, :]
    out[...] = (query[...] * response).astype(out.dtype)

    to_later(lambda d: rim_copy(d).wait_send())
    to_later(lambda d: pay_copy(d).wait_send())

    @pl.when(c + 1 < ctx)
    def _():
        query_copy().wait_send()

    sent = buf.at[pl.ds(0, count - 1)]
    pltpu.make_async_copy(sent, sent, send_sem.at[0]).wait()


def recv_count():
    passed = {p[:3] for p in PLAN if len(p) == 5 and p[1:3] != (0, 0)}
    return len(passed) + WIDE * DEEP


def on_device(tokens, in_weight, filter_taps, decay_rate, residue):
    count = lax.axis_size("tp")
    ctx = lax.axis_size("ctx")
    assert count == WIDE * DEEP
    operands = (tokens, jnp.transpose(in_weight, (1, 0, 2)), filter_taps, decay_rate, residue)
    hbm = pl.BlockSpec(memory_space=pltpu.MemorySpace.HBM)
    f32 = jnp.float32
    scratch = [
        pltpu.VMEM((count, ROWS, LANES), jnp.bfloat16),
        pltpu.VMEM((count, 3, LANES, LANES), jnp.bfloat16),
        pltpu.VMEM((3, ROWS, LANES), f32),
        pltpu.VMEM((3, 3, LANES), f32),
        pltpu.VMEM((MODES, LANES), f32),
        pltpu.VMEM((MODES, LANES), f32),
        pltpu.VMEM((MODES, ROWS, LANES), f32),
        pltpu.VMEM((MODES, ROWS, LANES), f32),
        pltpu.VMEM((HALO + ROWS, LANES), f32),
        pltpu.VMEM((8, ROWS // 8, 8, LANES), f32),
        pltpu.VMEM((3, HALO + ROWS, LANES), f32),
        pltpu.VMEM((HALO + ROWS, LANES), f32),
        pltpu.VMEM((8, ROWS, LANES), f32),
        pltpu.VMEM((ROWS, LANES), f32),
        pltpu.VMEM((ROWS, LANES), f32),
        pltpu.VMEM((MODES, LANES), f32),
        pltpu.VMEM((ctx - 1, MODES, LANES), f32),
        pltpu.VMEM((8, LANES), jnp.bfloat16),
        pltpu.VMEM((ctx - 1, 8, LANES), jnp.bfloat16),
        pltpu.VMEM((8, LANES), jnp.bfloat16),
        pltpu.VMEM((8, LANES), jnp.bfloat16),
        pltpu.SemaphoreType.DMA((4,)),
        pltpu.SemaphoreType.DMA((count // GROUP,)),
        pltpu.SemaphoreType.DMA((1,)),
        pltpu.SemaphoreType.DMA((recv_count(),)),
        pltpu.SemaphoreType.DMA((2 * ctx - 1,)),
        pltpu.SemaphoreType.DMA((2 * ctx - 1,)),
    ]

    def kernel(*refs):
        body(*refs)

    return pl.pallas_call(
        kernel,
        out_shape=jax.ShapeDtypeStruct((ROWS, LANES), jnp.bfloat16),
        in_specs=[hbm] * 5,
        out_specs=pl.BlockSpec(memory_space=pltpu.MemorySpace.VMEM),
        scratch_shapes=scratch,
        compiler_params=pltpu.CompilerParams(
            collective_id=0, has_side_effects=True, vmem_limit_bytes=48 * 1024 * 1024
        ),
        name="hyena",
    )(*(pltpu.with_memory_space_constraint(a, pltpu.MemorySpace.HBM) for a in operands))


def solution(mesh):
    return jax.shard_map(
        on_device,
        mesh=mesh,
        in_specs=(
            P("ctx", "tp"),
            P(None, None, "tp"),
            P(None, None, "tp"),
            P(None, "tp"),
            P(None, "tp"),
        ),
        out_specs=P("ctx", "tp"),
        check_vma=False,
    )
```

```python
import jax
import jax.numpy as jnp
from jax import lax
from jax.experimental import pallas as pl
from jax.experimental.pallas import tpu as pltpu
from jax.sharding import PartitionSpec as P

MESH = pl.DeviceIdType.MESH
PIECES = 2
PLAN = (
    (1, 0, 0, -1, 0), (1, 0, 0, 0, 1), (0, 0, 0, 0, -1), (0, 0), (1, 0, 0, 0, -1), (1, 0, 0, 1, 0), (0, 0, 0, 0, 1),
    (0, 0, 0, 0, 2), (0, 0, 0, 1, 0), (1, 0, 0, 0, -2), (0, 0, 0, -1, 0), (1, 0, 1, -1, 0), (0, 0, 7, 1, 0),
    (1, 3, 0, 0, -1), (1, 0, 1, 0, 1), (0, 3, 0, 0, 1), (1, 0, 7, 1, 0), (0, 3, 0, -1, 0), (0, 3, 0, 0, -1), (0, 1),
    (0, 7), (1, 0), (3, 0), (1, 1, 0, 0, 1), (0, 0, 1, 1, 0), (0, 0, 7, 0, -1), (1, 3, 0, -1, 0), (1, 0, 6, 0, -1),
    (1, 0, 6, 1, 0), (0, 0, 2, -1, 0), (0, 0, 2, 0, 1), (1, 0, 6, -1, 0), (0, 0, 2, 1, 0), (0, 0, 2, 0, 2),
    (1, 0, 6, 0, -2), (1, 0, 2, -1, 0), (0, 1, 7, 1, 0), (0, 2), (1, 0, 2, 0, 1), (1, 0, 2, 1, 0), (0, 1, 7, 0, -1),
    (0, 3, 1, -1, 0), (1, 7), (3, 1), (3, 7), (1, 1, 7, 1, 0), (0, 0, 6, 0, -1), (1, 2, 0, 0, 1), (0, 0, 6, -1, 0),
    (1, 1), (2, 0), (0, 3, 2, 0, 1), (1, 0, 5, 1, 0), (1, 0, 5, -1, 0), (1, 1, 6, 0, -2), (0, 6), (0, 1, 2, 0, 1),
    (0, 0, 4, 1, 0), (0, 0, 4, -1, 0), (0, 4), (1, 0, 4, -1, 0), (0, 1, 2, 1, 0), (1, 3, 2, 0, 1), (0, 2, 7, 0, -1),
    (1, 1, 6, 1, 0), (1, 3, 2, -1, 0), (1, 1, 2, 0, 1), (3, 2), (0, 1, 6, 0, -1), (0, 3), (1, 2), (1, 6),
    (0, 3, 6, 0, -1), (1, 2, 1, 0, 2), (0, 5), (2, 1), (2, 7), (3, 6), (0, 2, 7, 0, -2), (1, 1, 5, 1, 0),
    (0, 3, 3, -1, 0), (1, 1, 4, 1, 0), (0, 3, 4, -1, 0), (1, 4), (3, 3), (3, 4), (1, 3), (1, 5), (2, 2), (2, 6),
    (3, 5), (2, 3), (2, 4), (2, 5),
)
AHEAD = 16
FIRST_TABLE = 2
LANES = 256
ROWS = 128
MODES = 16
HALO = 8


WIDE, DEEP = 4, 8
GROUP = 4


def body(tokens, weight, taps_hbm, decay_hbm, residue_hbm, out, buf, wbuf, acc, taps, decay, residue,
         reversed_fall, read, kern, kern_rows, proj, source, shifted, inner, query, pay, inbox, rim, rim_in, query_rim, query_in,
         local_sem, weight_sem, send_sem, recv_sem, pay_send, pay_recv):
    count = WIDE * DEEP
    ctx = lax.axis_size("ctx")
    me = lax.axis_index("tp")
    c = lax.axis_index("ctx")
    my, mz = me // DEEP, lax.rem(me, DEEP)
    sends = [p for p in PLAN if len(p) == 5]
    blocks = [p for p in PLAN if len(p) == 2]
    piece = ROWS // PIECES
    turn = 1

    def at_offset(dy, dz):
        return lax.rem(my + turn * dy + 2 * WIDE, WIDE) * DEEP + lax.rem(mz + turn * dz + 2 * DEEP, DEEP)

    steps = sorted({p[3:] for p in sends})
    slots = {v: i for i, v in enumerate(blocks)}

    def slot(v):
        return slots[v]

    def weight_copy(v):
        rows = pl.ds(pl.multiple_of(at_offset(-v[0], -v[1]) * LANES, LANES), LANES)
        return pltpu.make_async_copy(weight.at[:, rows, :], wbuf.at[slot(v)], weight_sem.at[slot(v) // GROUP])

    def weight_wait(group):
        some = wbuf.at[pl.ds(group * GROUP, GROUP)]
        pltpu.make_async_copy(some, some, weight_sem.at[group]).wait()

    own = pltpu.make_async_copy(tokens, buf.at[0], local_sem.at[0])
    small = [
        pltpu.make_async_copy(taps_hbm, taps, local_sem.at[1]),
        pltpu.make_async_copy(decay_hbm, decay, local_sem.at[2]),
        pltpu.make_async_copy(residue_hbm, residue, local_sem.at[3]),
    ]

    barrier = pltpu.get_barrier_semaphore()
    for dy, dz in steps:
        pl.semaphore_signal(barrier, inc=1, device_id={"tp": at_offset(-dy, -dz)}, device_id_type=MESH)
    inbox[...] = jnp.zeros_like(inbox)
    rim_in[...] = jnp.zeros_like(rim_in)
    query_in[...] = jnp.zeros_like(query_in)
    query_rim[...] = jnp.zeros_like(query_rim)
    for d in range(1, ctx):
        @pl.when(c - d >= 0)
        def _(d=d):
            pl.semaphore_signal(barrier, inc=1, device_id={"ctx": c - d}, device_id_type=MESH)
    own.start()
    for copy in small:
        copy.start()
    for v in blocks[:AHEAD]:
        weight_copy(v).start()
    proj[:, 0:HALO, :] = jnp.zeros((3, HALO, LANES), jnp.float32)
    source[0:HALO, :] = jnp.zeros((HALO, LANES), jnp.float32)
    kern[...] = jnp.zeros_like(kern)
    own.wait()
    pl.semaphore_wait(barrier, len(steps) + ctx - 1 - c)

    passed = {(h, (y, z)) for h, y, z, _, _ in sends}
    kept = sorted(p for p in passed if p[1] != (0, 0))
    order_of = {p: i for i, p in enumerate(kept)}
    leaves = {v: [h for h in range(PIECES) if (h, v) not in passed] for v in blocks}

    leafy = [v for v in blocks if leaves[v] and v != (0, 0)]

    def recv_at(h, w):
        return recv_sem.at[order_of[h, w] if (h, w) in passed else len(kept) + leafy.index(w)]

    def piece_copy(step, h, v, w):
        rows = pl.ds(h * piece, piece)
        return pltpu.make_async_remote_copy(
            src_ref=buf.at[slot(v), rows],
            dst_ref=buf.at[slot(w), rows],
            send_sem=send_sem.at[0],
            recv_sem=recv_at(h, w),
            device_id={"tp": at_offset(*step)},
            device_id_type=MESH,
        )

    arrived = {(h, (0, 0)) for h in range(PIECES)}

    def await_piece(h, v):
        if (h, v) not in arrived:
            arrived.add((h, v))
            ref = buf.at[slot(v), pl.ds(h * piece, piece)]
            pltpu.make_async_copy(ref, ref, recv_at(h, v)).wait()

    def await_leaves(v):
        if leaves[v]:
            ref = buf.at[slot(v), pl.ds(0, piece * len(leaves[v]))]
            pltpu.make_async_copy(ref, ref, recv_at(leaves[v][0], v)).wait()

    def table(n):
        if n == 0:
            for copy in small:
                copy.wait()
        rate = decay[n : n + 1, :]
        coeff = residue[n : n + 1, :] * jnp.sqrt(1.0 - jnp.exp(-2.0 * rate))
        at = lax.broadcasted_iota(jnp.int32, (ROWS, LANES), 0).astype(jnp.float32)
        falling = jnp.exp(-rate * at)
        reversed_fall[n] = jnp.exp(-rate * (ROWS - 1.0 - at))
        read[n] = (coeff * jnp.exp(-rate)) * falling
        kern[HALO:, :] += coeff * falling

    def spread():
        @pl.loop(0, ROWS // 8)
        def _(q):
            rows = kern[pl.ds(pl.multiple_of(q * 8 + HALO, 8), 8), :]
            for r in range(8):
                kern_rows[r, q] = jnp.broadcast_to(rows[r : r + 1, :], (8, LANES))

    def multiply(order):
        pair = blocks[order - 1 : order + 1]
        for v in pair:
            for h in range(PIECES):
                if (h, v) in passed:
                    await_piece(h, v)
            await_leaves(v)
        if (order - 1) % GROUP == 0:
            weight_wait((order - 1) // GROUP)
        for s in range(3):
            part = sum(
                jnp.dot(buf[slot(v)], wbuf[slot(v), s], preferred_element_type=jnp.float32) for v in pair
            )
            if order == 1:
                acc[s] = part
            else:
                acc[s] += part

    tables = 0
    for p in PLAN:
        if len(p) == 5:
            h, v, step = p[0], p[1:3], p[3:]
            w = (v[0] + step[0]) % WIDE, (v[1] + step[1]) % DEEP
            await_piece(h, v)
            piece_copy(step, h, v, w).start()
            continue
        i = slot(p)
        if i + AHEAD < count:
            weight_copy(blocks[i + AHEAD]).start()
        if i % 2 == 1:
            multiply(i)
        if tables < MODES and i >= FIRST_TABLE:
            table(tables)
            tables += 1
            if tables == MODES:
                spread()

    def features(s, first, rows):
        at = first + HALO
        total = taps[0, s : s + 1, :] * proj[s, at : at + rows, :]
        total = total + taps[1, s : s + 1, :] * proj[s, at - 1 : at - 1 + rows, :]
        return total + taps[2, s : s + 1, :] * proj[s, at - 2 : at - 2 + rows, :]

    def project(s):
        rounded = acc[s].astype(jnp.bfloat16)
        proj[s, HALO:, :] = rounded.astype(jnp.float32)
        return rounded

    def copy_to(d, src, dst, index):
        return pltpu.make_async_remote_copy(
            src_ref=src,
            dst_ref=dst,
            send_sem=pay_send.at[index],
            recv_sem=pay_recv.at[index],
            device_id={"ctx": lax.rem(c + d, ctx)},
            device_id_type=MESH,
        )

    def rim_copy(d):
        return copy_to(d, rim, rim_in.at[d - 1], d - 1)

    def pay_copy(d):
        return copy_to(d, pay, inbox.at[d - 1], ctx - 1 + d - 1)

    def query_copy():
        return copy_to(1, query_rim, query_in, 2 * (ctx - 1))

    def to_later(act):
        for d in range(1, ctx):
            @pl.when(c + d < ctx)
            def _(d=d):
                act(d)

    def from_earlier(act):
        for d in range(1, ctx):
            @pl.when(c - d >= 0)
            def _(d=d):
                act(d)

    key, value = project(1), project(2)
    rim[...] = jnp.concatenate([key[0:2], key[ROWS - 2 :], value[0:2], value[ROWS - 2 :]], axis=0)
    to_later(lambda d: rim_copy(d).start())
    rows_in = lax.broadcasted_iota(jnp.int32, (ROWS, LANES), 0)
    late = jnp.where(rows_in >= 2, features(1, 0, ROWS) * features(2, 0, ROWS), 0.0)
    source[HALO:, :] = late
    for n in range(MODES):
        pay[n : n + 1, :] = jnp.sum(reversed_fall[n] * late, axis=0, keepdims=True)
    to_later(lambda d: pay_copy(d).start())
    query_rim[0:2, :] = project(0)[ROWS - 2 :]

    @pl.when(c + 1 < ctx)
    def _():
        query_copy().start()

    query[...] = features(0, 0, ROWS)
    for r in range(8):
        shifted[r] = source[HALO - r : HALO - r + ROWS, :]
    inner[...] = jnp.zeros_like(inner)

    @pl.loop(0, 8)
    def _(r):
        for half in range(LANES // 128):
            lanes = slice(half * 128, half * 128 + 128)
            late_rows = [shifted[r, 8 * i : 8 * i + 8, lanes] for i in range(ROWS // 8)]
            sums = [inner[8 * i : 8 * i + 8, lanes] for i in range(ROWS // 8)]
            for q in range(ROWS // 8):
                tap = kern_rows[r, q, :, lanes]
                for i in range(q, ROWS // 8):
                    sums[i] = sums[i] + tap * late_rows[i - q]
            for i in range(ROWS // 8):
                inner[8 * i : 8 * i + 8, lanes] = sums[i]

    rates = decay[...]
    over = jnp.exp(-rates * ROWS)
    from_first = jnp.exp(-rates * (ROWS - 1.0))
    from_second = jnp.exp(-rates * (ROWS - 2.0))

    from_earlier(lambda d: rim_copy(d).wait_recv())
    rims = [rim_in[d].astype(jnp.float32) for d in range(ctx - 1)]

    def lead(d, s):
        base = 4 * (s - 1)
        first, second = rims[d - 1][base : base + 1], rims[d - 1][base + 1 : base + 2]
        if d < ctx - 1:
            before, last = rims[d][base + 2 : base + 3], rims[d][base + 3 : base + 4]
        else:
            before = last = jnp.zeros((1, LANES), jnp.float32)
        t0, t1, t2 = (taps[j, s : s + 1, :] for j in range(3))
        return t0 * first + t1 * last + t2 * before, t0 * second + t1 * first + t2 * last

    state = jnp.zeros((MODES, LANES), jnp.float32)
    for d in range(ctx - 1, 0, -1):
        key_first, key_second = lead(d, 1)
        value_first, value_second = lead(d, 2)
        left = from_first * (key_first * value_first) + from_second * (key_second * value_second)
        state = over * state + left

    proj[1, HALO - 2 : HALO, :] = rims[0][2:4]
    proj[2, HALO - 2 : HALO, :] = rims[0][6:8]
    early = features(1, 0, 8) * features(2, 0, 8)
    inner[...] += kern[HALO:, :] * early[0:1, :] + kern[HALO - 1 : HALO - 1 + ROWS, :] * early[1:2, :]

    @pl.when(c > 0)
    def _():
        query_copy().wait_recv()

    proj[0, HALO - 2 : HALO, :] = query_in[0:2, :].astype(jnp.float32)
    query[0:8, :] = features(0, 0, 8)

    from_earlier(lambda d: pay_copy(d).wait_recv())
    others = jnp.zeros((MODES, LANES), jnp.float32)
    for d in range(ctx - 1, 0, -1):
        others = over * others + inbox[d - 1]
    state = state + others

    response = inner[...]
    for n in range(MODES):
        response = response + read[n] * state[n : n + 1, :]
    out[...] = (query[...] * response).astype(out.dtype)

    to_later(lambda d: rim_copy(d).wait_send())
    to_later(lambda d: pay_copy(d).wait_send())

    @pl.when(c + 1 < ctx)
    def _():
        query_copy().wait_send()

    sent = buf.at[pl.ds(0, count - 1)]
    pltpu.make_async_copy(sent, sent, send_sem.at[0]).wait()


def recv_count():
    passed = {p[:3] for p in PLAN if len(p) == 5}
    blocks = [p for p in PLAN if len(p) == 2 and p != (0, 0)]
    kept = sum(p[1:] != (0, 0) for p in passed)
    return kept + sum(any((h, *v) not in passed for h in range(PIECES)) for v in blocks)


def on_device(tokens, in_weight, filter_taps, decay_rate, residue):
    count = lax.axis_size("tp")
    ctx = lax.axis_size("ctx")
    assert count == WIDE * DEEP
    operands = (tokens, jnp.transpose(in_weight, (1, 0, 2)), filter_taps, decay_rate, residue)
    hbm = pl.BlockSpec(memory_space=pltpu.MemorySpace.HBM)
    f32 = jnp.float32
    scratch = [
        pltpu.VMEM((count, ROWS, LANES), jnp.bfloat16),
        pltpu.VMEM((count, 3, LANES, LANES), jnp.bfloat16),
        pltpu.VMEM((3, ROWS, LANES), f32),
        pltpu.VMEM((3, 3, LANES), f32),
        pltpu.VMEM((MODES, LANES), f32),
        pltpu.VMEM((MODES, LANES), f32),
        pltpu.VMEM((MODES, ROWS, LANES), f32),
        pltpu.VMEM((MODES, ROWS, LANES), f32),
        pltpu.VMEM((HALO + ROWS, LANES), f32),
        pltpu.VMEM((8, ROWS // 8, 8, LANES), f32),
        pltpu.VMEM((3, HALO + ROWS, LANES), f32),
        pltpu.VMEM((HALO + ROWS, LANES), f32),
        pltpu.VMEM((8, ROWS, LANES), f32),
        pltpu.VMEM((ROWS, LANES), f32),
        pltpu.VMEM((ROWS, LANES), f32),
        pltpu.VMEM((MODES, LANES), f32),
        pltpu.VMEM((ctx - 1, MODES, LANES), f32),
        pltpu.VMEM((8, LANES), jnp.bfloat16),
        pltpu.VMEM((ctx - 1, 8, LANES), jnp.bfloat16),
        pltpu.VMEM((8, LANES), jnp.bfloat16),
        pltpu.VMEM((8, LANES), jnp.bfloat16),
        pltpu.SemaphoreType.DMA((4,)),
        pltpu.SemaphoreType.DMA((count // GROUP,)),
        pltpu.SemaphoreType.DMA((1,)),
        pltpu.SemaphoreType.DMA((recv_count(),)),
        pltpu.SemaphoreType.DMA((2 * ctx - 1,)),
        pltpu.SemaphoreType.DMA((2 * ctx - 1,)),
    ]

    def kernel(*refs):
        body(*refs)

    return pl.pallas_call(
        kernel,
        out_shape=jax.ShapeDtypeStruct((ROWS, LANES), jnp.bfloat16),
        in_specs=[hbm] * 5,
        out_specs=pl.BlockSpec(memory_space=pltpu.MemorySpace.VMEM),
        scratch_shapes=scratch,
        compiler_params=pltpu.CompilerParams(
            collective_id=0, has_side_effects=True, vmem_limit_bytes=48 * 1024 * 1024
        ),
        name="hyena",
    )(*(pltpu.with_memory_space_constraint(a, pltpu.MemorySpace.HBM) for a in operands))


def solution(mesh):
    return jax.shard_map(
        on_device,
        mesh=mesh,
        in_specs=(
            P("ctx", "tp"),
            P(None, None, "tp"),
            P(None, None, "tp"),
            P(None, "tp"),
            P(None, "tp"),
        ),
        out_specs=P("ctx", "tp"),
        check_vma=False,
    )
```
